32 devices in a mesh: users: 16 (over z, x, core), ctx: 2 (over y).
Axes of the slice: x: 2, y: 2, z: 4, core: 2. Of those that a mesh axis runs over, the one named last changes fastest.
Arguments:
- events: bfloat16 [2048, 1024], P(('users', 'ctx')), may hold values from -6 to 6
- owner_id: int32 [2048, 1], P(('users', 'ctx')), may hold values from 0 to 15; in each aligned block of 64 rows (0 to 63, 64 to 127, ...) at most 6 rows name the same one
- event_bucket: int32 [2048], P(('users', 'ctx')), may hold values from 0 to 31
- cross_weight: bfloat16 [1024, 1024], P('users'), may hold values from -0.1875 to 0.1875
- cross_bias: float32 [1024], replicated, may hold values from -3 to 3
- project_weight: bfloat16 [1024, 4096], P('users'), may hold values from -0.1875 to 0.1875
- cache_keys: bfloat16 [16, 2048, 1024], P('users', 'ctx'), may hold values from -6 to 6
- cache_values: bfloat16 [16, 2048, 1024], P('users', 'ctx'), may hold values from -60 to 60
- cache_length: int32 [16], P('users'), may hold values from 256 to 2048
- cache_bucket: int32 [16, 2048], P('users', 'ctx'), may hold values from 0 to 31
- time_bias: float32 [32, 8], replicated, may hold values from -3 to 3
- norm_gain: float32 [1024], replicated, may hold values from 0.1 to 1.9
Outputs:
- gated: bfloat16 [2048, 1024], P(('users', 'ctx'))
The draws below stay inside these ranges and needn't reach their ends.
Inputs may be any that keep to these rules, and one draw needn't show every extreme that they name: `owner_id`: no user is named by more than 6 of the 64 rows of one ingestion shard, and some user reaches that.
All inputs are finite; a program needn't handle non-finite values.
Results may differ from the reference program's by a relative error of at most 0.035.
Values may be sent and summed in bfloat16 or wider, within the bound.
No kernel may reach another device: no remote copies, remote signals or barrier semaphores. Data moves between devices by JAX's collectives and lax.ppermute only.
A program may use at most 64 MiB of HBM per device.

```python
import math
import jax
import jax.numpy as jnp
import numpy as np
from jax import lax

D = 1024
H = 8
NB = 32
ROW_DEV = 64
CTX_DEV = 1024
USERS = 16
ROWS = 2048
CACHE = 2048
UCAP = 6
N_USERS = 16
N_CTX = 2


def draw_cache_values(key, part):
    base_key = jax.random.fold_in(jax.random.fold_in(key, 17), 0)
    values = jnp.clip(jax.random.normal(base_key, (USERS, CACHE, D), jnp.float32), -6.0, 6.0)
    return values.astype(jnp.bfloat16)


def set_ends(entries, own_key, smallest, largest):
    shape = entries.shape
    spot = [jax.random.randint(jax.random.fold_in(own_key, axis), (), 0, shape[axis]) for axis in range(len(shape))]
    entries = entries.at[tuple(spot)].set(smallest)
    longest = shape.index(max(shape))
    spot[longest] = (spot[longest] + 1) % shape[longest]
    return entries.at[tuple(spot)].set(largest)


def steps_of(own_key, extent, pieces, smallest, largest):
    loudness, own = 1.0, jax.random.fold_in(own_key, 6)
    for dim, blocks in pieces:
        steps = jnp.exp(jax.random.uniform(jax.random.fold_in(own, dim), (blocks,), jnp.float32, smallest / len(pieces), largest / len(pieces)))
        loudness = loudness * jnp.repeat(steps, extent[dim] // blocks).reshape([-1 if axis == dim else 1 for axis in range(len(extent))])
    return loudness


def routed_block(own_key, own, number, rows, number_of, top, most, slope):
    sequence = jax.random.permutation(own_key, number_of)
    crowded, ordinary = shares(number_of, rows * top, most, slope, True), shares(number_of, rows * top, most, slope, False)
    places = jnp.arange(number_of)

    def named(tallies, rotation):
        used = int((tallies > 0).sum())
        fixed = max(1, used // 4)
        passed = fixed + (places - fixed + rotation * (used - fixed)) % max(1, number_of - fixed)
        return jnp.zeros((number_of,), jnp.int32).at[sequence[jnp.where(places < fixed, places, passed)]].set(jnp.asarray(tallies, jnp.int32))

    tallies = jnp.where(number % 4 == 0, named(crowded, number // 4), named(ordinary, number - number // 4 - 1))
    mixed = jax.random.permutation(jax.random.fold_in(own, 3), number_of)
    donor, sink = mixed[0:number_of // 2 * 2:2], mixed[1:number_of // 2 * 2:2]
    margin = jnp.minimum(tallies[donor] - 1, most - tallies[sink]) // 2
    margin = jnp.where((donor == sequence[0]) | (sink == sequence[0]) | (tallies[sink] == 0), 0, jnp.maximum(margin, 0))
    passed = jax.random.randint(jax.random.fold_in(own, 4), (number_of // 2,), 0, 1 << 20) % (margin + 1)
    tallies = tallies.at[donor].add(-passed).at[sink].add(passed)
    items = jnp.searchsorted(jnp.cumsum(tallies), jnp.arange(rows * top), side="right").astype(jnp.int32)
    listing = items.reshape(top, rows).T
    listing = listing[jax.random.permutation(jax.random.fold_in(own, 1), rows)]
    rotation = jax.random.randint(jax.random.fold_in(own, 2), (rows, 1), 0, top)
    return jnp.take_along_axis(listing, (jnp.arange(top)[None, :] + rotation) % top, axis=1)


def shares(count, total, bound, skew, full):
    portions = [(1 << 20) // math.isqrt(grade ** skew) + 1 for grade in range(1, count + 1)]
    largest = bound if full else min(bound, max(-(-total // count), total * portions[0] // sum(portions)))
    least = 1 if total - largest >= count - 1 else 0
    holding, surplus = [largest] + [least] * (count - 1), total - largest - least * (count - 1)
    while surplus > 0:
        free = [i for i in range(1, count) if holding[i] < largest] or [i for i in range(1, count) if holding[i] < bound]
        mass, budget = sum([portions[i] for i in free]), surplus
        for i in free:
            addition = min(bound - holding[i], max(1, budget * portions[i] // mass), surplus)
            holding[i] = holding[i] + addition
            surplus = surplus - addition
    return np.array(holding)


def normal_values(own_key, dims, scale, most, cuts=(), kind=jnp.bfloat16):
    loudness = steps_of(own_key, dims, cuts, -0.22, 0.18) if cuts else 1.0
    result = jax.random.normal(own_key, dims, jnp.float32) * scale * loudness
    return jnp.minimum(jnp.maximum(result, -most), most).astype(kind)


def setup_inputs(seed: int = 0) -> dict:
    seeds = jax.random.split(jax.random.key(seed), 13)
    events = normal_values(seeds[0], (ROWS, D), 1.0, 6.0, ((0, 32),))
    owner_id_keys = jax.random.split(jax.random.fold_in(seeds[1], 1), ROWS // ROW_DEV)
    owner_id_turns = jax.random.permutation(jax.random.fold_in(seeds[1], 3), ROWS // ROW_DEV)
    owner_id = jax.vmap(lambda own, number: routed_block(jax.random.fold_in(seeds[1], 2), own, number, ROW_DEV, USERS, 1, UCAP, 2))(owner_id_keys, owner_id_turns).reshape((ROWS, 1))
    event_bucket = set_ends(jax.random.randint(seeds[2], (ROWS,), 0, NB), jax.random.fold_in(seeds[2], 1), 0, NB - 1).astype(jnp.int32)
    cross_weight = normal_values(seeds[3], (D, D), D ** -0.5, 0.1875, ((0, 16),))
    cross_bias = normal_values(seeds[4], (D,), 0.5, 3.0, (), jnp.float32)
    project_weight = normal_values(seeds[5], (D, 4 * D), D ** -0.5, 0.1875, ((0, 16),))
    cache_keys = normal_values(seeds[6], (USERS, CACHE, D), 1.0, 6.0, ((0, 16), (1, 2)))
    cache_values = draw_cache_values(jax.random.fold_in(seeds[12], 71), 0)
    cache_length = set_ends(jax.random.randint(seeds[8], (USERS,), CACHE // 8, CACHE + 1), jax.random.fold_in(seeds[8], 1), CACHE // 8, CACHE).astype(jnp.int32)
    cache_bucket = set_ends(jax.random.randint(seeds[9], (USERS, CACHE), 0, NB), jax.random.fold_in(seeds[9], 1), 0, NB - 1).astype(jnp.int32)
    time_bias = normal_values(seeds[10], (NB, H), 0.5, 3.0, (), jnp.float32)
    norm_gain = jnp.clip(1.0 + 0.18 * jax.random.normal(seeds[11], (D,), jnp.float32), 0.1, 1.9)
    return dict(events=events, owner_id=owner_id, event_bucket=event_bucket, cross_weight=cross_weight, cross_bias=cross_bias, project_weight=project_weight, cache_keys=cache_keys, cache_values=cache_values, cache_length=cache_length, cache_bucket=cache_bucket, time_bias=time_bias, norm_gain=norm_gain)


norm_epsilon = 1e-05
exact = lax.Precision.HIGHEST

def bias_table(buckets, time_bias):
    levels = jnp.arange(time_bias.shape[0], dtype=jnp.int32)
    picked = (buckets[:, None] == levels[None, :]).astype(jnp.float32)
    return jnp.dot(picked, time_bias.astype(jnp.float32), precision=exact)

def weighted_sum(keys_part, values_part, queries, key_bias, allowed, scale_factor):
    scores = jnp.einsum('khd,qhd->hkq', keys_part.astype(jnp.float32), queries.astype(jnp.float32), precision=exact)
    scores = scores * scale_factor + key_bias.T[:, :, None]
    weights = jnp.where(allowed, jax.nn.silu(scores), 0.0).astype(jnp.bfloat16)
    return jnp.einsum('hkq,khd->qhd', weights.astype(jnp.float32), values_part.astype(jnp.float32), precision=exact)

def reference(events, owner_id, event_bucket, cross_weight, cross_bias, project_weight, cache_keys, cache_values, cache_length, cache_bucket, time_bias, norm_gain):
    head_width = D // H
    device_count = N_USERS * N_CTX
    per_user = device_count * UCAP
    scale_factor = head_width ** (-0.5)
    source = events.astype(jnp.float32)
    crossing = jnp.dot(events, cross_weight, preferred_element_type=jnp.float32)
    crossed = (source * (crossing + cross_bias) + source).astype(jnp.bfloat16)
    owners = owner_id[:, 0].reshape(device_count, ROW_DEV)
    positions = jnp.arange(ROW_DEV, dtype=jnp.int32)
    earlier = (owners[:, None, :] == owners[:, :, None]) & (positions[None, None, :] < positions[None, :, None])
    ranking = lax.optimization_barrier(jnp.sum(earlier.astype(jnp.int32), axis=2))
    device_index = jnp.arange(device_count, dtype=jnp.int32)[:, None]
    slot_of_row = (owners * per_user + device_index * UCAP + ranking).reshape(-1).astype(jnp.int32)
    placed = jnp.zeros((USERS * per_user, D), jnp.bfloat16).at[slot_of_row].set(crossed)
    labels = jnp.zeros((USERS * per_user,), jnp.int32).at[slot_of_row].set(event_bucket + 1)
    slot_index = jnp.arange(per_user, dtype=jnp.int32)

    def one_user(bundle):
        user_rows, user_labels, keys_cache, values_cache, length, buckets_cache = bundle
        activated = jax.nn.silu(jnp.dot(user_rows, project_weight, preferred_element_type=jnp.float32))
        gate_units = activated[:, :D].astype(jnp.bfloat16)
        new_values = activated[:, D:2 * D].astype(jnp.bfloat16).reshape(N_USERS, N_CTX, UCAP, H, head_width)
        new_queries = activated[:, 2 * D:3 * D].astype(jnp.bfloat16).reshape(per_user, H, head_width)
        new_keys = activated[:, 3 * D:].astype(jnp.bfloat16).reshape(N_USERS, N_CTX, UCAP, H, head_width)
        key_valid = (user_labels > 0).reshape(N_USERS, N_CTX, UCAP)
        new_bias = bias_table(jnp.maximum(user_labels - 1, 0), time_bias).reshape(N_USERS, N_CTX, UCAP, H)
        cache_bias = bias_table(buckets_cache, time_bias)
        cache_live = jnp.arange(CACHE, dtype=jnp.int32) < length
        slot_order = slot_index.reshape(N_USERS, N_CTX, UCAP)
        attended = jnp.zeros((per_user, H, head_width), jnp.float32)
        for context in range(N_CTX):
            key_order = slot_order[:, context].reshape(-1)
            allowed = key_valid[:, context].reshape(-1)[None, :, None] & (key_order[None, :, None] <= slot_index[None, None, :])
            partial_value = weighted_sum(new_keys[:, context].reshape(-1, H, head_width), new_values[:, context].reshape(-1, H, head_width), new_queries, new_bias[:, context].reshape(-1, H), allowed, scale_factor)
            begin_cache = context * CTX_DEV
            partial_value = partial_value + weighted_sum(keys_cache[begin_cache:begin_cache + CTX_DEV].reshape(CTX_DEV, H, head_width), values_cache[begin_cache:begin_cache + CTX_DEV].reshape(CTX_DEV, H, head_width), new_queries, cache_bias[begin_cache:begin_cache + CTX_DEV], cache_live[begin_cache:begin_cache + CTX_DEV][None, :, None], scale_factor)
            rounded = lax.optimization_barrier(partial_value.astype(jnp.bfloat16))
            attended = attended + rounded.astype(jnp.float32)
        attended = attended.reshape(per_user, D)
        center = lax.optimization_barrier(jnp.mean(attended, axis=1, keepdims=True))
        spread = lax.optimization_barrier(jnp.mean(jnp.square(attended - center), axis=1, keepdims=True))
        normed = (attended - center) / jnp.sqrt(spread + norm_epsilon)
        return (normed * norm_gain * gate_units.astype(jnp.float32)).astype(jnp.bfloat16)
    results = lax.map(one_user, (placed.reshape(USERS, per_user, D), labels.reshape(USERS, per_user), cache_keys, cache_values, cache_length, cache_bucket))
    return results.reshape(USERS * per_user, D)[slot_of_row]
```

```python
import functools

import jax
import jax.numpy as jnp
import numpy as np
from jax import lax
from jax.experimental import pallas as pl
from jax.experimental.pallas import tpu as pltpu
from jax.sharding import PartitionSpec as P

H = 8
AXES = ("users", "ctx")
NORM_EPSILON = 1e-05
DEAD = -1e30
VMEM = pltpu.MemorySpace.VMEM
SMEM = pltpu.MemorySpace.SMEM


def round_up(value, step):
    return -(-value // step) * step


def bias_table(buckets, time_bias):
    levels = jnp.arange(time_bias.shape[0], dtype=jnp.int32)
    picked = (buckets[:, None] == levels[None, :]).astype(jnp.float32)
    return lax.dot_general(
        time_bias, picked, (((0,), (1,)), ((), ())), precision=lax.Precision.HIGHEST
    )


def cross_kernel(me_ref, *refs):
    head_count = H
    pieces = refs[:head_count]
    weights_ref, bias_ref, crossed_ref, meta_ref = refs[head_count : head_count + 4]
    me = me_ref[0]
    rows = pieces[0].shape[0]
    width = bias_ref.shape[1]
    head_width = width // head_count
    columns = pl.ds(pl.multiple_of(me * head_width, head_width), head_width)
    weights = weights_ref[:, :head_width]
    bias = bias_ref[:, columns]
    for mask in range(head_count):
        piece = pieces[mask]
        target = pl.ds(pl.multiple_of((me ^ mask) * rows, rows), rows)
        crossing = jnp.dot(piece[:, :width], weights, preferred_element_type=jnp.float32)
        source = piece[:, columns].astype(jnp.float32)
        crossed_ref[target, :] = (source * (crossing + bias) + source).astype(jnp.bfloat16)
        meta_ref[target, :] = piece[:, width:]


def project_kernel(slot_stride, kv_slots, chunk_users, me_ref, *refs):
    head_count = H
    pieces = refs[:head_count]
    weights_ref, meta_ref, base_ref, gate_ref, send_ref, rows_ref = refs[head_count:]
    me = me_ref[0]
    head_width = pieces[0].shape[1]
    for mask in range(head_count):
        columns = pl.ds(pl.multiple_of((me ^ mask) * head_width, head_width), head_width)
        rows_ref[:, columns] = pieces[mask][...]
    half = 0.5 * jnp.dot(
        rows_ref[...], weights_ref[:, head_width:], preferred_element_type=jnp.float32
    )
    activated = (half * (1.0 + jnp.tanh(half))).astype(jnp.bfloat16)
    gate_ref[...] = activated[:, :head_width]
    meta = meta_ref[...]
    turned = meta.astype(jnp.float32).T
    owner = turned[0:1, :].astype(jnp.int32)
    rank = turned[1:2, :].astype(jnp.int32)
    slot_of_row = owner * slot_stride + rank + base_ref[...]
    labels = jnp.broadcast_to(meta[:, 2:3].astype(jnp.float32), meta.shape).astype(jnp.bfloat16)
    carried = jnp.concatenate([labels, activated[:, head_width:]], axis=1)
    context_count = slot_stride // kv_slots
    user_count = send_ref.shape[0] // context_count
    chunk = chunk_users * slot_stride
    lane = lax.broadcasted_iota(jnp.int32, (8, head_width), 1)
    for first in range(0, user_count, chunk_users):
        slots = lax.broadcasted_iota(jnp.int32, (chunk, slot_of_row.shape[1]), 0) + first * slot_stride
        picked = (slots == slot_of_row).astype(jnp.float32).astype(jnp.bfloat16)
        placed = jnp.dot(picked, carried, preferred_element_type=jnp.float32)
        for user in range(chunk_users):
            low = user * slot_stride
            queries = placed[low : low + slot_stride, 2 * head_width : 3 * head_width]
            for context in range(context_count):
                target = (first + user) * context_count + context
                start = low + context * kv_slots
                part = placed[start : start + kv_slots]
                send_ref[target, 0:slot_stride, :] = queries.astype(jnp.bfloat16)
                at = slot_stride
                send_ref[target, at : at + kv_slots, :] = part[:, 3 * head_width :].astype(
                    jnp.bfloat16
                )
                at += kv_slots
                send_ref[target, at : at + kv_slots, :] = part[
                    :, head_width : 2 * head_width
                ].astype(jnp.bfloat16)
                at += kv_slots
                note = part[0:8, :head_width]
                for tile in range(1, kv_slots // 8):
                    note = jnp.where(lane == tile, part[tile * 8 : tile * 8 + 8, :head_width], note)
                send_ref[target, at : at + 8, :] = note.astype(jnp.bfloat16)


def attend_kernel(
    slot_stride,
    kv_slots,
    half_scale,
    recv_ref,
    keys_ref,
    values_ref,
    cache_bias_ref,
    time_bias_ref,
    key_order_ref,
    query_order_ref,
    out_ref,
):
    head = pl.program_id(0)
    group_count = recv_ref.shape[0]
    head_width = recv_ref.shape[3]
    block_rows = out_ref.shape[0]
    block_groups = block_rows // slot_stride
    first = pl.program_id(1) * block_groups
    queries = recv_ref[pl.ds(first, block_groups), 0, 0:slot_stride, :].reshape(
        block_rows, head_width
    )
    nt = (((1,), (1,)), ((), ()))
    scores = lax.dot_general(queries, keys_ref[...], nt, preferred_element_type=jnp.float32)
    half = scores * half_scale + cache_bias_ref[pl.ds(head, 1), :]
    weights = (half * (1.0 + jnp.tanh(half))).astype(jnp.bfloat16)
    summed = jnp.dot(weights, values_ref[...], preferred_element_type=jnp.float32)
    at = slot_stride
    key_count = group_count * kv_slots
    new_keys = recv_ref[:, 0, at : at + kv_slots, :].reshape(key_count, head_width)
    at += kv_slots
    new_values = recv_ref[:, 0, at : at + kv_slots, :].reshape(key_count, head_width)
    at += kv_slots
    notes = recv_ref[:, 0, at : at + 8, :].astype(jnp.float32)
    buckets = jnp.concatenate(
        [notes[g, :, t : t + 1] for g in range(group_count) for t in range(kv_slots // 8)], axis=0
    ).astype(jnp.int32)
    table = time_bias_ref[pl.ds(head, 1), :]
    levels = lax.broadcasted_iota(jnp.int32, (key_count, table.shape[1]), 1)
    new_bias = jnp.sum(jnp.where(levels == buckets, table, 0.0), axis=1, keepdims=True)
    new_scores = lax.dot_general(new_keys, queries, nt, preferred_element_type=jnp.float32)
    new_half = new_scores * half_scale + 0.5 * new_bias
    new_weights = jnp.where(
        key_order_ref[...] <= query_order_ref[...], new_half * (1.0 + jnp.tanh(new_half)), 0.0
    ).astype(jnp.bfloat16)
    summed = summed + lax.dot_general(
        new_weights, new_values, (((0,), (0,)), ((), ())), preferred_element_type=jnp.float32
    )
    out_ref[...] = summed.astype(jnp.bfloat16)


def shards(
    events,
    owner_id,
    event_bucket,
    cross_weight,
    cross_bias,
    project_weight,
    cache_keys,
    cache_values,
    cache_length,
    cache_bucket,
    time_bias,
    norm_gain,
):
    row_count, width = events.shape
    head_width = width // H
    owner_count = lax.axis_size("users")
    context_count = lax.axis_size("ctx")
    device_count = owner_count * context_count
    inner = H // context_count
    group_count = owner_count // inner
    user_index, context_index = lax.axis_index("users"), lax.axis_index("ctx")
    me = (user_index % inner) * context_count + context_index
    capacity = max(2, (3 * row_count + 2 * owner_count - 1) // (2 * owner_count))
    kv_slots = round_up(inner * capacity, 8)
    slot_stride = context_count * kv_slots
    cache_rows = cache_keys.shape[1]
    bucket_count = time_bias.shape[0]
    group_rows = H * row_count
    core = context_count if inner > 1 else 0
    blocks = project_weight.shape[1] // width

    def swap(block, mask):
        pairs = [(d, d // H * H + (d % H ^ mask)) for d in range(device_count)]
        return lax.ppermute(block, AXES, pairs)

    def spread(block):
        pieces = [block] + [None] * (H - 1)
        for mask in range(1, H):
            if not mask & core:
                pieces[mask] = swap(block, mask)
        for mask in range(H):
            if mask & core:
                pieces[mask] = swap(pieces[mask ^ core], core)
        return pieces

    owners = owner_id[:, 0]
    positions = jnp.arange(row_count, dtype=jnp.int32)
    earlier = (owners[None, :] == owners[:, None]) & (positions[None, :] < positions[:, None])
    ranking = jnp.sum(earlier.astype(jnp.int32), axis=1)
    lanes = jnp.arange(head_width, dtype=jnp.int32)[None, :]
    meta = jnp.where(
        lanes == 0,
        owners[:, None],
        jnp.where(lanes == 1, ranking[:, None], jnp.where(lanes == 2, event_bucket[:, None], 0)),
    ).astype(jnp.bfloat16)
    pieces = spread(jnp.concatenate([events, meta], axis=1))

    def head_columns(matrix):
        split = matrix.reshape(row_count_of(matrix), -1, inner, context_count, head_width)
        mine = lax.dynamic_index_in_dim(split, context_index, 3, keepdims=False)
        return mine.transpose(2, 0, 1, 3).reshape(inner, matrix.shape[0], -1)

    def row_count_of(matrix):
        return matrix.shape[0]

    columns = jnp.concatenate([head_columns(cross_weight), head_columns(project_weight)], axis=2)
    columns = jnp.broadcast_to(columns[None], (group_count,) + columns.shape)
    columns = columns.reshape((owner_count,) + columns.shape[2:])
    weights = lax.all_to_all(columns, "users", split_axis=0, concat_axis=0, tiled=True)
    weights = weights.reshape(width, (1 + blocks) * head_width)

    me_scalar = me.astype(jnp.int32).reshape(1)
    vmem_spec = pl.BlockSpec(memory_space=VMEM)
    smem_spec = pl.BlockSpec(memory_space=SMEM)
    crossed, group_meta = pl.pallas_call(
        cross_kernel,
        out_shape=(
            jax.ShapeDtypeStruct((group_rows, head_width), jnp.bfloat16),
            jax.ShapeDtypeStruct((group_rows, head_width), jnp.bfloat16),
        ),
        in_specs=[smem_spec] + [vmem_spec] * (H + 2),
        out_specs=(vmem_spec, vmem_spec),
        name="cross",
    )(me_scalar, *pieces, weights, cross_bias[None, :])
    crossed_pieces = spread(crossed)

    shard = np.arange(group_rows) // row_count
    base = ((shard % context_count) * kv_slots + (shard // context_count) * capacity)[None, :]
    message_rows = slot_stride + 2 * kv_slots + 8
    chunk_users = max(1, min(owner_count, 512 // slot_stride))
    while owner_count % chunk_users:
        chunk_users -= 1
    gate, outgoing = pl.pallas_call(
        functools.partial(project_kernel, slot_stride, kv_slots, chunk_users),
        out_shape=(
            jax.ShapeDtypeStruct((group_rows, head_width), jnp.bfloat16),
            jax.ShapeDtypeStruct((device_count, message_rows, head_width), jnp.bfloat16),
        ),
        in_specs=[smem_spec] + [vmem_spec] * (H + 3),
        out_specs=(vmem_spec, vmem_spec),
        scratch_shapes=[pltpu.VMEM((group_rows, width), jnp.bfloat16)],
        name="project",
    )(me_scalar, *crossed_pieces, weights, group_meta, jnp.asarray(base, jnp.int32))

    teams = [list(range(g * H, (g + 1) * H)) for g in range(group_count)]
    gate_rows = lax.all_to_all(
        gate.reshape(H, row_count, head_width),
        AXES,
        split_axis=0,
        concat_axis=0,
        tiled=True,
        axis_index_groups=teams,
    )
    arrived = lax.all_to_all(outgoing, AXES, split_axis=0, concat_axis=0, tiled=True)
    arrived = arrived.reshape(group_count, H, message_rows, head_width)

    live = jnp.arange(cache_rows, dtype=jnp.int32) < cache_length[0] - context_index * cache_rows
    cache_bias = jnp.where(live[None, :], 0.5 * bias_table(cache_bucket[0], time_bias), DEAD)

    def order_of(group, context, rest):
        member = rest // capacity * context_count + context
        return (group * H + member) * capacity + rest % capacity

    slots = np.arange(group_count * slot_stride)
    query_order = order_of(slots // slot_stride, slots % slot_stride // kv_slots, slots % kv_slots)
    slots = np.arange(group_count * kv_slots)
    key_order = (
        jnp.asarray(order_of(slots // kv_slots, 0, slots % kv_slots), jnp.int32)
        + context_index * capacity
    )
    block_groups = max(1, min(group_count, 256 // slot_stride))
    while group_count % block_groups:
        block_groups -= 1
    block_rows = block_groups * slot_stride
    query_rows = group_count * slot_stride
    partials = pl.pallas_call(
        functools.partial(attend_kernel, slot_stride, kv_slots, 0.5 * head_width**-0.5),
        out_shape=jax.ShapeDtypeStruct((query_rows, width), jnp.bfloat16),
        grid=(H, query_rows // block_rows),
        in_specs=[
            pl.BlockSpec((group_count, 1, message_rows, head_width), lambda h, b: (0, h, 0, 0)),
            pl.BlockSpec((cache_rows, head_width), lambda h, b: (0, h)),
            pl.BlockSpec((cache_rows, head_width), lambda h, b: (0, h)),
            pl.BlockSpec((H, cache_rows), lambda h, b: (0, 0)),
            pl.BlockSpec((H, bucket_count), lambda h, b: (0, 0)),
            pl.BlockSpec((group_count * kv_slots, 1), lambda h, b: (0, 0)),
            pl.BlockSpec((1, block_rows), lambda h, b: (0, b)),
        ],
        out_specs=pl.BlockSpec((block_rows, head_width), lambda h, b: (b, h)),
        name="attend",
    )(
        arrived,
        cache_keys[0],
        cache_values[0],
        cache_bias,
        time_bias.T,
        key_order[:, None],
        jnp.asarray(query_order, jnp.int32)[None, :],
    )

    real = partials.reshape(group_count, context_count, kv_slots, width)[:, :, : inner * capacity]
    real = real.reshape(group_count, context_count, inner, capacity, width).transpose(0, 2, 1, 3, 4)
    returned = lax.all_to_all(
        real.reshape(device_count, capacity, width), AXES, split_axis=0, concat_axis=0, tiled=True
    ).reshape(device_count * capacity, width)
    sources = jnp.arange(device_count * capacity, dtype=jnp.int32)
    source_owner = sources // (context_count * capacity)
    picked = (source_owner[None, :] == owners[:, None]) & (
        sources[None, :] % capacity == ranking[:, None]
    )
    attended = jnp.dot(picked.astype(jnp.bfloat16), returned, preferred_element_type=jnp.float32)
    center = jnp.mean(attended, axis=1, keepdims=True)
    spread_out = jnp.mean(jnp.square(attended - center), axis=1, keepdims=True)
    normed = (attended - center) * lax.rsqrt(spread_out + NORM_EPSILON)
    gate_units = gate_rows.transpose(1, 0, 2).reshape(row_count, width).astype(jnp.float32)
    return (normed * norm_gain * gate_units).astype(jnp.bfloat16)


def solution(mesh):
    return jax.shard_map(
        shards,
        mesh=mesh,
        in_specs=(
            P(AXES, None),
            P(AXES, None),
            P(AXES),
            P("users", None),
            P(),
            P("users", None),
            P("users", "ctx", None),
            P("users", "ctx", None),
            P("users"),
            P("users", "ctx"),
            P(),
            P(),
        ),
        out_specs=P(AXES, None),
        check_vma=False,
    )
```

```python
import functools

import jax
import jax.numpy as jnp
import numpy as np
from jax import lax
from jax.experimental import pallas as pl
from jax.experimental.pallas import tpu as pltpu
from jax.sharding import PartitionSpec as P

H = 8
AXES = ("users", "ctx")
NORM_EPSILON = 1e-05
DEAD = -1e30
VMEM = pltpu.MemorySpace.VMEM
SMEM = pltpu.MemorySpace.SMEM


def round_up(value, step):
    return -(-value // step) * step


def bias_table(buckets, time_bias):
    levels = jnp.arange(time_bias.shape[0], dtype=jnp.int32)
    picked = (buckets[:, None] == levels[None, :]).astype(jnp.float32)
    return lax.dot_general(
        time_bias, picked, (((0,), (1,)), ((), ())), precision=lax.Precision.HIGHEST
    )


def pick_columns(inner, context_count, head_width, context, matrix_ref, columns_ref):
    owner_count, _, picked = columns_ref.shape
    blocks = picked // head_width
    width = matrix_ref.shape[1] // blocks
    for turn in range(inner):
        for block in range(blocks):
            start = block * width + (turn * context_count + context) * head_width
            piece = matrix_ref[:, pl.ds(pl.multiple_of(start, head_width), head_width)]
            for first in range(0, owner_count, inner):
                lanes = slice(block * head_width, (block + 1) * head_width)
                columns_ref[first + turn, :, lanes] = piece


def prepare_kernel(
    inner,
    context_count,
    context_ref,
    events_ref,
    owner_ref,
    bucket_ref,
    matrix_ref,
    packed_ref,
    columns_ref,
):
    rows, width = events_ref.shape
    head_width = packed_ref.shape[1] - width
    across = owner_ref[...].astype(jnp.float32)
    owners = jnp.broadcast_to(across, (head_width, rows)).T
    lane = lax.broadcasted_iota(jnp.int32, (rows, rows), 1)
    line = lax.broadcasted_iota(jnp.int32, (rows, rows), 0)
    earlier = (across == owners[:, :1]) & (lane < line)
    ranking = jnp.sum(jnp.where(earlier, 1.0, 0.0), axis=1, keepdims=True)
    buckets = jnp.broadcast_to(bucket_ref[...].astype(jnp.float32), (head_width, rows)).T
    lanes = lax.broadcasted_iota(jnp.int32, (rows, head_width), 1)
    meta = jnp.where(lanes == 0, owners, jnp.where(lanes == 1, ranking, buckets))
    packed_ref[:, :width] = events_ref[...]
    packed_ref[:, width:] = jnp.where(lanes < 3, meta, 0.0).astype(jnp.bfloat16)
    pick_columns(inner, context_count, head_width, context_ref[0], matrix_ref, columns_ref)


def spread_columns_kernel(inner, context_count, head_width, context_ref, matrix_ref, columns_ref):
    pick_columns(inner, context_count, head_width, context_ref[0], matrix_ref, columns_ref)


def grant(*arrays):
    held = sum(int(np.prod(a.shape)) * a.dtype.itemsize for a in arrays)
    return pltpu.CompilerParams(vmem_limit_bytes=min(60 << 20, 2 * held + (6 << 20)))


def pick_columns(inner, context_count, head_width, context, matrix_ref, columns_ref):
    owner_count, _, picked = columns_ref.shape
    blocks = picked // head_width
    width = matrix_ref.shape[1] // blocks
    for turn in range(inner):
        for block in range(blocks):
            start = block * width + (turn * context_count + context) * head_width
            piece = matrix_ref[:, pl.ds(pl.multiple_of(start, head_width), head_width)]
            for first in range(0, owner_count, inner):
                lanes = slice(block * head_width, (block + 1) * head_width)
                columns_ref[first + turn, :, lanes] = piece


def prepare_kernel(
    inner,
    context_count,
    context_ref,
    events_ref,
    owner_ref,
    bucket_ref,
    matrix_ref,
    packed_ref,
    columns_ref,
):
    rows, width = events_ref.shape
    head_width = packed_ref.shape[1] - width
    across = owner_ref[...].astype(jnp.float32)
    owners = jnp.broadcast_to(across, (head_width, rows)).T
    lane = lax.broadcasted_iota(jnp.int32, (rows, rows), 1)
    line = lax.broadcasted_iota(jnp.int32, (rows, rows), 0)
    earlier = (across == owners[:, :1]) & (lane < line)
    ranking = jnp.sum(jnp.where(earlier, 1.0, 0.0), axis=1, keepdims=True)
    buckets = jnp.broadcast_to(bucket_ref[...].astype(jnp.float32), (head_width, rows)).T
    lanes = lax.broadcasted_iota(jnp.int32, (rows, head_width), 1)
    meta = jnp.where(lanes == 0, owners, jnp.where(lanes == 1, ranking, buckets))
    packed_ref[:, :width] = events_ref[...]
    packed_ref[:, width:] = jnp.where(lanes < 3, meta, 0.0).astype(jnp.bfloat16)
    pick_columns(inner, context_count, head_width, context_ref[0], matrix_ref, columns_ref)


def spread_columns_kernel(inner, context_count, head_width, context_ref, matrix_ref, columns_ref):
    pick_columns(inner, context_count, head_width, context_ref[0], matrix_ref, columns_ref)


def grant(*arrays):
    held = sum(int(np.prod(a.shape)) * a.dtype.itemsize for a in arrays)
    return pltpu.CompilerParams(vmem_limit_bytes=min(60 << 20, 2 * held + (6 << 20)))


def fetch(copies, sems):
    started = [pltpu.make_async_copy(*pair, sems.at[i]) for i, pair in enumerate(copies)]
    for copy in started:
        copy.start()
    return started


def cross_kernel(me_ref, *refs):
    head_count = H
    pieces = refs[:head_count]
    matrix_ref, bias_ref, crossed_ref, meta_ref = refs[head_count:]
    me = me_ref[0]
    rows = pieces[0].shape[0]
    width = bias_ref.shape[1]
    head_width = width // head_count
    columns = pl.ds(pl.multiple_of(me * head_width, head_width), head_width)
    matrix = matrix_ref[...]
    bias = bias_ref[:, columns]
    for mask in range(head_count):
        piece = pieces[mask]
        target = pl.ds(pl.multiple_of((me ^ mask) * rows, rows), rows)
        crossing = jnp.dot(piece[:, :width], matrix, preferred_element_type=jnp.float32)
        source = piece[:, columns].astype(jnp.float32)
        crossed_ref[target, :] = (source * (crossing + bias) + source).astype(jnp.bfloat16)
        meta_ref[target, :] = piece[:, width:]


def project_kernel(slot_stride, kv_slots, chunk_users, me_ref, *refs):
    head_count = H
    pieces = refs[:head_count]
    matrix_ref, meta_ref, base_ref = refs[head_count : head_count + 3]
    gate_refs = refs[head_count + 3 : 2 * head_count + 3]
    send_ref, rows_ref, gate_ref = refs[2 * head_count + 3 :]
    me = me_ref[0]
    head_width = pieces[0].shape[1]
    for mask in range(head_count):
        columns = pl.ds(pl.multiple_of((me ^ mask) * head_width, head_width), head_width)
        rows_ref[:, columns] = pieces[mask][...]
    meta = meta_ref[...]
    turned = meta.astype(jnp.float32).T
    owner = turned[0:1, :].astype(jnp.int32)
    rank = turned[1:2, :].astype(jnp.int32)
    slot_of_row = owner * slot_stride + rank + base_ref[...]
    labels = jnp.broadcast_to(meta[:, 2:3].astype(jnp.float32), meta.shape).astype(jnp.bfloat16)
    half = 0.5 * jnp.dot(rows_ref[...], matrix_ref[...], preferred_element_type=jnp.float32)
    activated = (half * (1.0 + jnp.tanh(half))).astype(jnp.bfloat16)
    gate_ref[...] = activated[:, :head_width]
    shard_rows = gate_refs[0].shape[0]
    for mask in range(head_count):
        source = pl.ds(pl.multiple_of((me ^ mask) * shard_rows, shard_rows), shard_rows)
        gate_refs[mask][...] = gate_ref[source, :]
    carried = jnp.concatenate([labels, activated[:, head_width:]], axis=1)
    context_count = slot_stride // kv_slots
    user_count = send_ref.shape[0] // context_count
    chunk = chunk_users * slot_stride
    lane = lax.broadcasted_iota(jnp.int32, (8, head_width), 1)
    for first in range(0, user_count, chunk_users):
        slots = lax.broadcasted_iota(jnp.int32, (chunk, slot_of_row.shape[1]), 0)
        picked = (slots + first * slot_stride == slot_of_row).astype(jnp.float32)
        placed = jnp.dot(
            picked.astype(jnp.bfloat16), carried, preferred_element_type=jnp.float32
        )
        for user in range(chunk_users):
            low = user * slot_stride
            queries = placed[low : low + slot_stride, 2 * head_width : 3 * head_width]
            queries = queries.astype(jnp.bfloat16)
            for context in range(context_count):
                target = (first + user) * context_count + context
                start = low + context * kv_slots
                part = placed[start : start + kv_slots]
                send_ref[target, 0:slot_stride, :] = queries
                at = slot_stride
                send_ref[target, at : at + kv_slots, :] = part[:, 3 * head_width :].astype(
                    jnp.bfloat16
                )
                at += kv_slots
                send_ref[target, at : at + kv_slots, :] = part[
                    :, head_width : 2 * head_width
                ].astype(jnp.bfloat16)
                at += kv_slots
                note = part[0:8, :head_width]
                for tile in range(1, kv_slots // 8):
                    note = jnp.where(lane == tile, part[tile * 8 : tile * 8 + 8, :head_width], note)
                send_ref[target, at : at + 8, :] = note.astype(jnp.bfloat16)


def attend_kernel(
    slot_stride,
    kv_slots,
    block_groups,
    half_scale,
    arrived_ref,
    all_keys_ref,
    all_values_ref,
    cache_bias_ref,
    time_bias_ref,
    key_order_ref,
    query_order_ref,
    out_ref,
    summed_ref,
    recv_ref,
    keys_ref,
    values_ref,
    sems,
):
    copies = []
    for head in range(recv_ref.shape[1]):
        part = pl.ds(head * recv_ref.shape[3], recv_ref.shape[3])
        copies.append((arrived_ref.at[:, head], recv_ref.at[:, head]))
        copies.append((all_keys_ref.at[:, part], keys_ref.at[:, part]))
        copies.append((all_values_ref.at[:, part], values_ref.at[:, part]))
    started = fetch(copies, sems)
    group_count, head_count, _, head_width = recv_ref.shape
    context_count = slot_stride // kv_slots
    inner = head_count // context_count
    capacity = out_ref.shape[1] // head_count
    block_rows = block_groups * slot_stride
    key_count = group_count * kv_slots
    nt = (((1,), (1,)), ((), ()))
    tn = (((0,), (0,)), ((), ()))

    def one_block(block, waits):
        first = block * block_groups
        for head in range(head_count):
            if waits:
                for copy in started[3 * head : 3 * head + 3]:
                    copy.wait()
            columns = slice(head * head_width, (head + 1) * head_width)
            queries = recv_ref[pl.ds(first, block_groups), head, 0:slot_stride, :]
            queries = queries.reshape(block_rows, head_width)
            scores = lax.dot_general(
                queries, keys_ref[:, columns], nt, preferred_element_type=jnp.float32
            )
            half = scores * half_scale + cache_bias_ref[head : head + 1, :]
            weights = (half * (1.0 + jnp.tanh(half))).astype(jnp.bfloat16)
            summed = jnp.dot(weights, values_ref[:, columns], preferred_element_type=jnp.float32)
            at = slot_stride
            new_keys = recv_ref[:, head, at : at + kv_slots, :].reshape(key_count, head_width)
            at += kv_slots
            new_values = recv_ref[:, head, at : at + kv_slots, :].reshape(key_count, head_width)
            at += kv_slots
            notes = recv_ref[:, head, at : at + 8, :].astype(jnp.float32)
            buckets = jnp.concatenate(
                [notes[g, :, t : t + 1] for g in range(group_count) for t in range(kv_slots // 8)],
                axis=0,
            ).astype(jnp.int32)
            table = time_bias_ref[head : head + 1, :]
            levels = lax.broadcasted_iota(jnp.int32, (key_count, table.shape[1]), 1)
            new_bias = jnp.sum(jnp.where(levels == buckets, table, 0.0), axis=1, keepdims=True)
            new_scores = lax.dot_general(new_keys, queries, nt, preferred_element_type=jnp.float32)
            new_half = new_scores * half_scale + 0.5 * new_bias
            new_weights = jnp.where(
                key_order_ref[...] <= query_order_ref[pl.ds(block, 1), :],
                new_half * (1.0 + jnp.tanh(new_half)),
                0.0,
            ).astype(jnp.bfloat16)
            summed = summed + lax.dot_general(
                new_weights, new_values, tn, preferred_element_type=jnp.float32
            )
            summed_ref[pl.ds(head, block_rows, stride=head_count), :] = summed
        for group in range(block_groups):
            for context in range(context_count):
                for turn in range(inner):
                    slot = (group * context_count + context) * kv_slots + turn * capacity
                    rows = slice(slot * head_count, (slot + capacity) * head_count)
                    target = (first + group) * head_count + turn * context_count + context
                    out_ref[target] = summed_ref[rows, :].astype(jnp.bfloat16)

    block_count = group_count // block_groups
    if block_count == 1:
        one_block(0, True)
    else:
        for copy in started:
            copy.wait()

        def step(block, carry):
            one_block(block, False)
            return carry

        lax.fori_loop(0, block_count, step, 0)


def finish_kernel(me_ref, place_ref, *refs):
    head_count = H
    gates = refs[:head_count]
    returned_ref, gain_ref, out_ref, tall_ref, gate_ref = refs[head_count:]
    me = me_ref[0]
    rows, width = out_ref.shape
    head_width = width // head_count
    for mask in range(head_count):
        columns = pl.ds(pl.multiple_of((me ^ mask) * head_width, head_width), head_width)
        gate_ref[:, columns] = gates[mask][...]
    for row in range(rows):
        total = returned_ref[place_ref[row, 0]].astype(jnp.float32)
        for context in range(1, place_ref.shape[1]):
            total = total + returned_ref[place_ref[row, context]].astype(jnp.float32)
        tall_ref[row * head_count : (row + 1) * head_count, :] = total
    attended = jnp.concatenate(
        [tall_ref[pl.ds(head, rows, stride=head_count), :] for head in range(head_count)], axis=1
    )
    center = jnp.mean(attended, axis=1, keepdims=True)
    moved = attended - center
    spread = jnp.mean(jnp.square(moved), axis=1, keepdims=True)
    normed = moved * lax.rsqrt(spread + NORM_EPSILON)
    out_ref[...] = (normed * gain_ref[...] * gate_ref[...].astype(jnp.float32)).astype(jnp.bfloat16)


def shards(
    events,
    owner_id,
    event_bucket,
    cross_weight,
    cross_bias,
    project_weight,
    cache_keys,
    cache_values,
    cache_length,
    cache_bucket,
    time_bias,
    norm_gain,
):
    row_count, width = events.shape
    head_width = width // H
    owner_count = lax.axis_size("users")
    context_count = lax.axis_size("ctx")
    device_count = owner_count * context_count
    inner = H // context_count
    group_count = owner_count // inner
    user_index, context_index = lax.axis_index("users"), lax.axis_index("ctx")
    me = (user_index % inner) * context_count + context_index
    capacity = max(2, (3 * row_count + 2 * owner_count - 1) // (2 * owner_count))
    kv_slots = round_up(inner * capacity, 8)
    slot_stride = context_count * kv_slots
    cache_rows = cache_keys.shape[1]
    group_rows = H * row_count
    core = context_count if inner > 1 else 0
    blocks = project_weight.shape[1] // width

    def swap(block, mask):
        pairs = [(d, d // H * H + (d % H ^ mask)) for d in range(device_count)]
        return lax.ppermute(block, AXES, pairs)

    def spread(block):
        pieces = [block] + [None] * (H - 1)
        for mask in range(1, H):
            if not mask & core:
                pieces[mask] = swap(block, mask)
        for mask in range(H):
            if mask & core:
                pieces[mask] = swap(pieces[mask ^ core], core)
        return pieces

    owners = owner_id[:, 0]
    positions = jnp.arange(row_count, dtype=jnp.int32)
    earlier = (owners[None, :] == owners[:, None]) & (positions[None, :] < positions[:, None])
    ranking = jnp.sum(earlier.astype(jnp.int32), axis=1)
    vmem_spec = pl.BlockSpec(memory_space=VMEM)
    smem_spec = pl.BlockSpec(memory_space=SMEM)
    any_spec = pl.BlockSpec(memory_space=pl.ANY)
    me_scalar = me.astype(jnp.int32).reshape(1)
    context_scalar = context_index.astype(jnp.int32).reshape(1)
    packed_shape = jax.ShapeDtypeStruct((row_count, width + head_width), jnp.bfloat16)
    matrix_rows = cross_weight.shape[0]
    cross_shape = jax.ShapeDtypeStruct((owner_count, matrix_rows, head_width), jnp.bfloat16)
    packed, cross_columns = pl.pallas_call(
        functools.partial(prepare_kernel, inner, context_count),
        out_shape=(packed_shape, cross_shape),
        in_specs=[smem_spec] + [vmem_spec] * 4,
        out_specs=(vmem_spec, vmem_spec),
        name="prepare",
    )(context_scalar, events, owner_id.reshape(1, -1), event_bucket[None, :], cross_weight)
    pieces = spread(packed)
    project_shape = jax.ShapeDtypeStruct(
        (owner_count, matrix_rows, blocks * head_width), jnp.bfloat16
    )
    project_columns = pl.pallas_call(
        functools.partial(spread_columns_kernel, inner, context_count, head_width),
        out_shape=project_shape,
        in_specs=[smem_spec, vmem_spec],
        out_specs=vmem_spec,
        compiler_params=grant(project_shape),
        name="columns",
    )(context_scalar, project_weight)

    cross_columns = lax.all_to_all(cross_columns, "users", split_axis=0, concat_axis=0, tiled=True)
    project_columns = lax.all_to_all(
        project_columns, "users", split_axis=0, concat_axis=0, tiled=True
    )
    project_columns = project_columns.reshape(width, blocks * head_width)
    cross_columns = cross_columns.reshape(width, head_width)

    crossed, group_meta = pl.pallas_call(
        cross_kernel,
        out_shape=(
            jax.ShapeDtypeStruct((group_rows, head_width), jnp.bfloat16),
            jax.ShapeDtypeStruct((group_rows, head_width), jnp.bfloat16),
        ),
        in_specs=[smem_spec] + [vmem_spec] * (H + 2),
        out_specs=(vmem_spec, vmem_spec),
        compiler_params=grant(*pieces, cross_columns),
        name="cross",
    )(me_scalar, *pieces, cross_columns, cross_bias[None, :])
    crossed_pieces = spread(crossed)

    shard = np.arange(group_rows) // row_count
    base = ((shard % context_count) * kv_slots + (shard // context_count) * capacity)[None, :]
    message_rows = slot_stride + 2 * kv_slots + 8
    chunk_users = max(1, min(owner_count, 512 // slot_stride))
    while owner_count % chunk_users:
        chunk_users -= 1
    messages = jax.ShapeDtypeStruct((device_count, message_rows, head_width), jnp.bfloat16)
    *gates, outgoing = pl.pallas_call(
        functools.partial(project_kernel, slot_stride, kv_slots, chunk_users),
        out_shape=[jax.ShapeDtypeStruct((row_count, head_width), jnp.bfloat16)] * H
        + [messages],
        in_specs=[smem_spec] + [vmem_spec] * (H + 3),
        out_specs=[vmem_spec] * (H + 1),
        scratch_shapes=[
            pltpu.VMEM((group_rows, width), jnp.bfloat16),
            pltpu.VMEM((group_rows, head_width), jnp.bfloat16),
        ],
        compiler_params=grant(*crossed_pieces, project_columns, messages, messages),
        name="project",
    )(me_scalar, *crossed_pieces, project_columns, group_meta, jnp.asarray(base, jnp.int32))
    gates = [gates[0]] + [swap(gates[mask], mask) for mask in range(1, H)]

    arrived = lax.all_to_all(outgoing, AXES, split_axis=0, concat_axis=0, tiled=True)
    arrived = arrived.reshape(group_count, H, message_rows, head_width)

    live = jnp.arange(cache_rows, dtype=jnp.int32) < cache_length[0] - context_index * cache_rows
    cache_bias = jnp.where(live[None, :], 0.5 * bias_table(cache_bucket[0], time_bias), DEAD)

    def order_of(group, context, rest):
        member = rest // capacity * context_count + context
        return (group * H + member) * capacity + rest % capacity

    slots = np.arange(group_count * slot_stride)
    query_order = order_of(slots // slot_stride, slots % slot_stride // kv_slots, slots % kv_slots)
    slots = np.arange(group_count * kv_slots)
    key_order = (
        jnp.asarray(order_of(slots // kv_slots, 0, slots % kv_slots), jnp.int32)
        + context_index * capacity
    )
    block_groups = max(1, min(group_count, 256 // slot_stride))
    while group_count % block_groups:
        block_groups -= 1
    block_rows = block_groups * slot_stride
    partials = pl.pallas_call(
        functools.partial(
            attend_kernel, slot_stride, kv_slots, block_groups, 0.5 * head_width**-0.5
        ),
        out_shape=jax.ShapeDtypeStruct((device_count, capacity * H, head_width), jnp.bfloat16),
        in_specs=[any_spec] * 3 + [vmem_spec] * 4,
        out_specs=vmem_spec,
        scratch_shapes=[
            pltpu.VMEM((block_rows * H, head_width), jnp.float32),
            pltpu.VMEM(arrived.shape, arrived.dtype),
            pltpu.VMEM(cache_keys.shape[1:], cache_keys.dtype),
            pltpu.VMEM(cache_values.shape[1:], cache_values.dtype),
            pltpu.SemaphoreType.DMA((3 * H,)),
        ],
        name="attend",
    )(
        arrived,
        cache_keys[0],
        cache_values[0],
        cache_bias,
        time_bias.T,
        key_order[:, None],
        jnp.asarray(query_order, jnp.int32).reshape(-1, block_rows),
    )

    returned = lax.all_to_all(partials, AXES, split_axis=0, concat_axis=0, tiled=True)
    contexts = jnp.arange(context_count, dtype=jnp.int32)[None, :]
    places = (owners[:, None] * context_count + contexts) * capacity + ranking[:, None]
    return pl.pallas_call(
        finish_kernel,
        out_shape=jax.ShapeDtypeStruct((row_count, width), jnp.bfloat16),
        in_specs=[smem_spec] * 2 + [vmem_spec] * (H + 2),
        out_specs=vmem_spec,
        scratch_shapes=[
            pltpu.VMEM((row_count * H, head_width), jnp.float32),
            pltpu.VMEM((row_count, width), jnp.bfloat16),
        ],
        compiler_params=grant(returned, norm_gain),
        name="finish",
    )(
        me_scalar,
        places,
        *gates,
        returned.reshape(device_count * capacity, H, head_width),
        norm_gain[None, :],
    )


def solution(mesh):
    return jax.shard_map(
        shards,
        mesh=mesh,
        in_specs=(
            P(AXES, None),
            P(AXES, None),
            P(AXES),
            P("users", None),
            P(),
            P("users", None),
            P("users", "ctx", None),
            P("users", "ctx", None),
            P("users"),
            P("users", "ctx"),
            P(),
            P(),
        ),
        out_specs=P(AXES, None),
        check_vma=False,
    )
```

```python
import functools

import jax
import jax.numpy as jnp
import numpy as np
from jax import lax
from jax.experimental import pallas as pl
from jax.experimental.pallas import tpu as pltpu
from jax.sharding import PartitionSpec as P

H = 8
AXES = ("users", "ctx")
NORM_EPSILON = 1e-05
DEAD = -1e30
VMEM = pltpu.MemorySpace.VMEM
SMEM = pltpu.MemorySpace.SMEM


def round_up(value, step):
    return -(-value // step) * step


def grant(*arrays):
    held = sum(int(np.prod(a.shape)) * a.dtype.itemsize for a in arrays)
    return pltpu.CompilerParams(vmem_limit_bytes=min(60 << 20, 2 * held + (6 << 20)))


def pick_columns(inner, context_count, head_width, context, matrix_ref, columns_ref):
    owner_count, _, picked = columns_ref.shape
    blocks = picked // head_width
    width = matrix_ref.shape[1] // blocks
    for turn in range(inner):
        for block in range(blocks):
            start = block * width + (turn * context_count + context) * head_width
            piece = matrix_ref[:, pl.ds(pl.multiple_of(start, head_width), head_width)]
            for first in range(0, owner_count, inner):
                lanes = slice(block * head_width, (block + 1) * head_width)
                columns_ref[first + turn, :, lanes] = piece


def prepare_kernel(
    inner,
    context_count,
    context_ref,
    events_ref,
    owner_ref,
    bucket_ref,
    matrix_ref,
    packed_ref,
    columns_ref,
):
    rows, width = events_ref.shape
    head_width = packed_ref.shape[1] - width
    across = owner_ref[...].astype(jnp.float32)
    owners = jnp.broadcast_to(across, (head_width, rows)).T
    lane = lax.broadcasted_iota(jnp.int32, (rows, rows), 1)
    line = lax.broadcasted_iota(jnp.int32, (rows, rows), 0)
    earlier = (across == owners[:, :1]) & (lane < line)
    ranking = jnp.sum(jnp.where(earlier, 1.0, 0.0), axis=1, keepdims=True)
    buckets = jnp.broadcast_to(bucket_ref[...].astype(jnp.float32), (head_width, rows)).T
    lanes = lax.broadcasted_iota(jnp.int32, (rows, head_width), 1)
    meta = jnp.where(lanes == 0, owners, jnp.where(lanes == 1, ranking, buckets))
    packed_ref[:, :width] = events_ref[...]
    packed_ref[:, width:] = jnp.where(lanes < 3, meta, 0.0).astype(jnp.bfloat16)
    pick_columns(inner, context_count, head_width, context_ref[0], matrix_ref, columns_ref)


def spread_columns_kernel(inner, context_count, head_width, context_ref, matrix_ref, columns_ref):
    pick_columns(inner, context_count, head_width, context_ref[0], matrix_ref, columns_ref)


def grant(*arrays):
    held = sum(int(np.prod(a.shape)) * a.dtype.itemsize for a in arrays)
    return pltpu.CompilerParams(vmem_limit_bytes=min(60 << 20, 2 * held + (6 << 20)))


def cross_kernel(me_ref, *refs):
    head_count = H
    pieces = refs[:head_count]
    matrix_ref, bias_ref, crossed_ref, meta_ref = refs[head_count:]
    me = me_ref[0]
    rows = pieces[0].shape[0]
    width = bias_ref.shape[1]
    head_width = width // head_count
    columns = pl.ds(pl.multiple_of(me * head_width, head_width), head_width)
    matrix = matrix_ref[...]
    bias = bias_ref[:, columns]
    for mask in range(head_count):
        piece = pieces[mask]
        target = pl.ds(pl.multiple_of((me ^ mask) * rows, rows), rows)
        crossing = jnp.dot(piece[:, :width], matrix, preferred_element_type=jnp.float32)
        source = piece[:, columns].astype(jnp.float32)
        crossed_ref[target, :] = (source * (crossing + bias) + source).astype(jnp.bfloat16)
        meta_ref[target, :] = piece[:, width:]


def project_kernel(slot_stride, kv_slots, chunk_users, me_ref, *refs):
    head_count = H
    pieces = refs[:head_count]
    matrix_ref, meta_ref, base_ref = refs[head_count : head_count + 3]
    gate_refs = refs[head_count + 3 : 2 * head_count + 3]
    out_ref, rows_ref, gate_ref, send_ref, sems = refs[2 * head_count + 3 :]
    me = me_ref[0]
    head_width = pieces[0].shape[1]
    for mask in range(head_count):
        columns = pl.ds(pl.multiple_of((me ^ mask) * head_width, head_width), head_width)
        rows_ref[:, columns] = pieces[mask][...]
    meta = meta_ref[...]
    turned = meta.astype(jnp.float32).T
    owner = turned[0:1, :].astype(jnp.int32)
    rank = turned[1:2, :].astype(jnp.int32)
    slot_of_row = owner * slot_stride + rank + base_ref[...]
    labels = jnp.broadcast_to(meta[:, 2:3].astype(jnp.float32), meta.shape).astype(jnp.bfloat16)
    half = 0.5 * jnp.dot(rows_ref[...], matrix_ref[...], preferred_element_type=jnp.float32)
    activated = (half * (1.0 + jnp.tanh(half))).astype(jnp.bfloat16)
    gate_ref[...] = activated[:, :head_width]
    shard_rows = gate_refs[0].shape[0]
    for mask in range(head_count):
        source = pl.ds(pl.multiple_of((me ^ mask) * shard_rows, shard_rows), shard_rows)
        gate_refs[mask][...] = gate_ref[source, :]
    carried = jnp.concatenate([labels, activated[:, head_width:]], axis=1)
    context_count = slot_stride // kv_slots
    user_count = send_ref.shape[0] // context_count
    chunk = chunk_users * slot_stride
    lane = lax.broadcasted_iota(jnp.int32, (8, head_width), 1)
    started = []
    for turn, first in enumerate(range(0, user_count, chunk_users)):
        slots = lax.broadcasted_iota(jnp.int32, (chunk, slot_of_row.shape[1]), 0)
        picked = (slots + first * slot_stride == slot_of_row).astype(jnp.float32)
        placed = jnp.dot(
            picked.astype(jnp.bfloat16), carried, preferred_element_type=jnp.float32
        )
        for user in range(chunk_users):
            low = user * slot_stride
            queries = placed[low : low + slot_stride, 2 * head_width : 3 * head_width]
            queries = queries.astype(jnp.bfloat16)
            for context in range(context_count):
                target = (first + user) * context_count + context
                start = low + context * kv_slots
                part = placed[start : start + kv_slots]
                send_ref[target, 0:slot_stride, :] = queries
                at = slot_stride
                send_ref[target, at : at + kv_slots, :] = part[:, 3 * head_width :].astype(
                    jnp.bfloat16
                )
                at += kv_slots
                send_ref[target, at : at + kv_slots, :] = part[
                    :, head_width : 2 * head_width
                ].astype(jnp.bfloat16)
                at += kv_slots
                note = part[0:8, :head_width]
                for tile in range(1, kv_slots // 8):
                    note = jnp.where(lane == tile, part[tile * 8 : tile * 8 + 8, :head_width], note)
                send_ref[target, at : at + 8, :] = note.astype(jnp.bfloat16)
        done = pl.ds(first * context_count, chunk_users * context_count)
        copy = pltpu.make_async_copy(send_ref.at[done], out_ref.at[done], sems.at[turn])
        copy.start()
        started.append(copy)
    for copy in started:
        copy.wait()


def stage_kernel(
    live_ref,
    after_ref,
    far_ref,
    bucket_ref,
    time_bias_ref,
    key_order_ref,
    query_order_ref,
    near_ref,
    cache_bias_ref,
    near_time_bias_ref,
    near_key_order_ref,
    near_query_order_ref,
    sem,
):
    copy = pltpu.make_async_copy(far_ref, near_ref, sem)
    copy.start()
    table = time_bias_ref[...]
    shape = (table.shape[1], bucket_ref.shape[1])
    levels = lax.broadcasted_iota(jnp.int32, shape, 0)
    picked = jnp.where(levels == bucket_ref[...], 1.0, 0.0)
    bias = jnp.dot(
        table, picked, precision=lax.Precision.HIGHEST, preferred_element_type=jnp.float32
    )
    positions = lax.broadcasted_iota(jnp.int32, bias.shape, 1)
    cache_bias_ref[...] = jnp.where(positions < live_ref[0], 0.5 * bias, DEAD)
    near_time_bias_ref[...] = table
    near_key_order_ref[...] = key_order_ref[...]
    near_query_order_ref[...] = query_order_ref[...]
    copy.wait()


def attend_kernel(
    slot_stride,
    kv_slots,
    block_groups,
    half_scale,
    recv_ref,
    keys_ref,
    far_values_ref,
    cache_bias_ref,
    time_bias_ref,
    key_order_ref,
    query_order_ref,
    out_ref,
    summed_ref,
    values_ref,
    weights_ref,
    sem,
):
    copy = pltpu.make_async_copy(far_values_ref, values_ref, sem)
    copy.start()
    group_count, head_count, _, head_width = recv_ref.shape
    context_count = slot_stride // kv_slots
    inner = head_count // context_count
    capacity = out_ref.shape[1] // head_count
    block_rows = block_groups * slot_stride
    key_count = group_count * kv_slots
    nt = (((1,), (1,)), ((), ()))
    tn = (((0,), (0,)), ((), ()))

    def weigh(first, head):
        columns = slice(head * head_width, (head + 1) * head_width)
        queries = recv_ref[pl.ds(first, block_groups), head, 0:slot_stride, :]
        queries = queries.reshape(block_rows, head_width)
        scores = lax.dot_general(
            queries, keys_ref[:, columns], nt, preferred_element_type=jnp.float32
        )
        half = scores * half_scale + cache_bias_ref[head : head + 1, :]
        weights_ref[head] = (half * (1.0 + jnp.tanh(half))).astype(jnp.bfloat16)

    def gather(block, first, head):
        columns = slice(head * head_width, (head + 1) * head_width)
        queries = recv_ref[pl.ds(first, block_groups), head, 0:slot_stride, :]
        queries = queries.reshape(block_rows, head_width)
        summed = jnp.dot(
            weights_ref[head], values_ref[:, columns], preferred_element_type=jnp.float32
        )
        at = slot_stride
        new_keys = recv_ref[:, head, at : at + kv_slots, :].reshape(key_count, head_width)
        at += kv_slots
        new_values = recv_ref[:, head, at : at + kv_slots, :].reshape(key_count, head_width)
        at += kv_slots
        notes = recv_ref[:, head, at : at + 8, :].astype(jnp.float32)
        buckets = jnp.concatenate(
            [notes[g, :, t : t + 1] for g in range(group_count) for t in range(kv_slots // 8)],
            axis=0,
        ).astype(jnp.int32)
        table = time_bias_ref[head : head + 1, :]
        levels = lax.broadcasted_iota(jnp.int32, (key_count, table.shape[1]), 1)
        new_bias = jnp.sum(jnp.where(levels == buckets, table, 0.0), axis=1, keepdims=True)
        new_scores = lax.dot_general(new_keys, queries, nt, preferred_element_type=jnp.float32)
        new_half = new_scores * half_scale + 0.5 * new_bias
        new_weights = jnp.where(
            key_order_ref[...] <= query_order_ref[pl.ds(block, 1), :],
            new_half * (1.0 + jnp.tanh(new_half)),
            0.0,
        ).astype(jnp.bfloat16)
        summed = summed + lax.dot_general(
            new_weights, new_values, tn, preferred_element_type=jnp.float32
        )
        summed_ref[pl.ds(head, block_rows, stride=head_count), :] = summed

    def one_block(block, waits):
        first = block * block_groups
        lag = head_count // 2
        for head in range(head_count + lag):
            if head < head_count:
                weigh(first, head)
            if waits and head == lag:
                copy.wait()
            if head >= lag:
                gather(block, first, head - lag)
        for group in range(block_groups):
            for context in range(context_count):
                for turn in range(inner):
                    slot = (group * context_count + context) * kv_slots + turn * capacity
                    rows = slice(slot * head_count, (slot + capacity) * head_count)
                    target = (first + group) * head_count + turn * context_count + context
                    out_ref[target] = summed_ref[rows, :].astype(jnp.bfloat16)

    block_count = group_count // block_groups
    if block_count == 1:
        one_block(0, True)
    else:
        copy.wait()

        def step(block, carry):
            one_block(block, False)
            return carry

        lax.fori_loop(0, block_count, step, 0)


def finish_kernel(me_ref, place_ref, *refs):
    head_count = H
    gates = refs[:head_count]
    returned_ref, gain_ref, out_ref, tall_ref, gate_ref = refs[head_count:]
    me = me_ref[0]
    rows, width = out_ref.shape
    head_width = width // head_count
    for mask in range(head_count):
        columns = pl.ds(pl.multiple_of((me ^ mask) * head_width, head_width), head_width)
        gate_ref[:, columns] = gates[mask][...]
    for row in range(rows):
        total = returned_ref[place_ref[row, 0]].astype(jnp.float32)
        for context in range(1, place_ref.shape[1]):
            total = total + returned_ref[place_ref[row, context]].astype(jnp.float32)
        tall_ref[row * head_count : (row + 1) * head_count, :] = total
    attended = jnp.concatenate(
        [tall_ref[pl.ds(head, rows, stride=head_count), :] for head in range(head_count)], axis=1
    )
    center = jnp.mean(attended, axis=1, keepdims=True)
    moved = attended - center
    spread = jnp.mean(jnp.square(moved), axis=1, keepdims=True)
    normed = moved * lax.rsqrt(spread + NORM_EPSILON)
    out_ref[...] = (normed * gain_ref[...] * gate_ref[...].astype(jnp.float32)).astype(jnp.bfloat16)


def shards(
    events,
    owner_id,
    event_bucket,
    cross_weight,
    cross_bias,
    project_weight,
    cache_keys,
    cache_values,
    cache_length,
    cache_bucket,
    time_bias,
    norm_gain,
):
    row_count, width = events.shape
    head_width = width // H
    owner_count = lax.axis_size("users")
    context_count = lax.axis_size("ctx")
    device_count = owner_count * context_count
    inner = H // context_count
    group_count = owner_count // inner
    user_index, context_index = lax.axis_index("users"), lax.axis_index("ctx")
    me = (user_index % inner) * context_count + context_index
    capacity = max(2, (3 * row_count + 2 * owner_count - 1) // (2 * owner_count))
    kv_slots = round_up(inner * capacity, 8)
    slot_stride = context_count * kv_slots
    cache_rows = cache_keys.shape[1]
    bucket_count = time_bias.shape[0]
    group_rows = H * row_count
    core = context_count if inner > 1 else 0
    blocks = project_weight.shape[1] // width

    def swap(block, mask):
        pairs = [(d, d // H * H + (d % H ^ mask)) for d in range(device_count)]
        return lax.ppermute(block, AXES, pairs)

    def spread(block):
        pieces = [block] + [None] * (H - 1)
        for mask in range(1, H):
            if not mask & core:
                pieces[mask] = swap(block, mask)
        for mask in range(H):
            if mask & core:
                pieces[mask] = swap(pieces[mask ^ core], core)
        return pieces

    owners = owner_id[:, 0]
    positions = jnp.arange(row_count, dtype=jnp.int32)
    earlier = (owners[None, :] == owners[:, None]) & (positions[None, :] < positions[:, None])
    ranking = jnp.sum(earlier.astype(jnp.int32), axis=1)
    vmem_spec = pl.BlockSpec(memory_space=VMEM)
    smem_spec = pl.BlockSpec(memory_space=SMEM)
    hbm_spec = pl.BlockSpec(memory_space=pltpu.MemorySpace.HBM)
    me_scalar = me.astype(jnp.int32).reshape(1)
    context_scalar = context_index.astype(jnp.int32).reshape(1)
    packed_shape = jax.ShapeDtypeStruct((row_count, width + head_width), jnp.bfloat16)
    matrix_rows = cross_weight.shape[0]
    cross_shape = jax.ShapeDtypeStruct((owner_count, matrix_rows, head_width), jnp.bfloat16)
    packed, cross_columns = pl.pallas_call(
        functools.partial(prepare_kernel, inner, context_count),
        out_shape=(packed_shape, cross_shape),
        in_specs=[smem_spec] + [vmem_spec] * 4,
        out_specs=(vmem_spec, vmem_spec),
        name="prepare",
    )(context_scalar, events, owner_id.reshape(1, -1), event_bucket[None, :], cross_weight)
    pieces = spread(packed)
    project_shape = jax.ShapeDtypeStruct(
        (owner_count, matrix_rows, blocks * head_width), jnp.bfloat16
    )
    project_columns = pl.pallas_call(
        functools.partial(spread_columns_kernel, inner, context_count, head_width),
        out_shape=project_shape,
        in_specs=[smem_spec, vmem_spec],
        out_specs=vmem_spec,
        compiler_params=grant(project_shape),
        name="columns",
    )(context_scalar, project_weight)

    cross_columns = lax.all_to_all(cross_columns, "users", split_axis=0, concat_axis=0, tiled=True)
    project_columns = lax.all_to_all(
        project_columns, "users", split_axis=0, concat_axis=0, tiled=True
    )
    project_columns = project_columns.reshape(width, blocks * head_width)
    cross_columns = cross_columns.reshape(width, head_width)

    crossed, group_meta = pl.pallas_call(
        cross_kernel,
        out_shape=(
            jax.ShapeDtypeStruct((group_rows, head_width), jnp.bfloat16),
            jax.ShapeDtypeStruct((group_rows, head_width), jnp.bfloat16),
        ),
        in_specs=[smem_spec] + [vmem_spec] * (H + 2),
        out_specs=(vmem_spec, vmem_spec),
        compiler_params=grant(*pieces, cross_columns),
        name="cross",
    )(me_scalar, *pieces, cross_columns, cross_bias[None, :])
    crossed_pieces = spread(crossed)

    shard = np.arange(group_rows) // row_count
    base = ((shard % context_count) * kv_slots + (shard // context_count) * capacity)[None, :]
    message_rows = slot_stride + 2 * kv_slots + 8
    chunk_users = max(1, min(owner_count, 512 // slot_stride))
    while owner_count % chunk_users:
        chunk_users -= 1
    messages = jax.ShapeDtypeStruct((device_count, message_rows, head_width), jnp.bfloat16)
    *gates, outgoing = pl.pallas_call(
        functools.partial(project_kernel, slot_stride, kv_slots, chunk_users),
        out_shape=[jax.ShapeDtypeStruct((row_count, head_width), jnp.bfloat16)] * H
        + [messages],
        in_specs=[smem_spec] + [vmem_spec] * (H + 3),
        out_specs=[vmem_spec] * H + [hbm_spec],
        scratch_shapes=[
            pltpu.VMEM((group_rows, width), jnp.bfloat16),
            pltpu.VMEM((group_rows, head_width), jnp.bfloat16),
            pltpu.VMEM(messages.shape, messages.dtype),
            pltpu.SemaphoreType.DMA((owner_count // chunk_users,)),
        ],
        compiler_params=grant(*crossed_pieces, project_columns, messages, messages),
        name="project",
    )(me_scalar, *crossed_pieces, project_columns, group_meta, jnp.asarray(base, jnp.int32))
    gates = [gates[0]] + [swap(gates[mask], mask) for mask in range(1, H)]

    arrived = lax.all_to_all(outgoing, AXES, split_axis=0, concat_axis=0, tiled=True)
    arrived = arrived.reshape(group_count, H, message_rows, head_width)

    def order_of(group, context, rest):
        member = rest // capacity * context_count + context
        return (group * H + member) * capacity + rest % capacity

    slots = np.arange(group_count * slot_stride)
    query_order = order_of(slots // slot_stride, slots % slot_stride // kv_slots, slots % kv_slots)
    slots = np.arange(group_count * kv_slots)
    key_order = (
        jnp.asarray(order_of(slots // kv_slots, 0, slots % kv_slots), jnp.int32)
        + context_index * capacity
    )
    block_groups = max(1, min(group_count, 256 // slot_stride))
    while group_count % block_groups:
        block_groups -= 1
    block_rows = block_groups * slot_stride
    live = (cache_length[0] - context_index * cache_rows).astype(jnp.int32).reshape(1)
    query_order = jnp.asarray(query_order, jnp.int32).reshape(-1, block_rows)

    def far(cache):
        return pltpu.with_memory_space_constraint(cache[0], pltpu.MemorySpace.HBM)

    near = pl.pallas_call(
        stage_kernel,
        out_shape=(
            jax.ShapeDtypeStruct(cache_keys.shape[1:], cache_keys.dtype),
            jax.ShapeDtypeStruct((H, cache_rows), jnp.float32),
            jax.ShapeDtypeStruct((H, bucket_count), jnp.float32),
            jax.ShapeDtypeStruct((group_count * kv_slots, 1), jnp.int32),
            jax.ShapeDtypeStruct(query_order.shape, jnp.int32),
        ),
        in_specs=[smem_spec, vmem_spec, hbm_spec] + [vmem_spec] * 4,
        out_specs=[vmem_spec] * 5,
        scratch_shapes=[pltpu.SemaphoreType.DMA(())],
        compiler_params=grant(cache_keys),
        name="stage",
    )(live, gates[0], far(cache_keys), cache_bucket, time_bias.T, key_order[:, None], query_order)

    partials = pl.pallas_call(
        functools.partial(
            attend_kernel, slot_stride, kv_slots, block_groups, 0.5 * head_width**-0.5
        ),
        out_shape=jax.ShapeDtypeStruct((device_count, capacity * H, head_width), jnp.bfloat16),
        in_specs=[vmem_spec] * 2 + [hbm_spec] + [vmem_spec] * 4,
        out_specs=vmem_spec,
        scratch_shapes=[
            pltpu.VMEM((block_rows * H, head_width), jnp.float32),
            pltpu.VMEM(cache_values.shape[1:], cache_values.dtype),
            pltpu.VMEM((H, block_rows, cache_rows), jnp.bfloat16),
            pltpu.SemaphoreType.DMA(()),
        ],
        compiler_params=grant(arrived, cache_keys, cache_values, query_order),
        name="attend",
    )(arrived, near[0], far(cache_values), *near[1:])

    returned = lax.all_to_all(partials, AXES, split_axis=0, concat_axis=0, tiled=True)
    contexts = jnp.arange(context_count, dtype=jnp.int32)[None, :]
    places = (owners[:, None] * context_count + contexts) * capacity + ranking[:, None]
    return pl.pallas_call(
        finish_kernel,
        out_shape=jax.ShapeDtypeStruct((row_count, width), jnp.bfloat16),
        in_specs=[smem_spec] * 2 + [vmem_spec] * (H + 2),
        out_specs=vmem_spec,
        scratch_shapes=[
            pltpu.VMEM((row_count * H, head_width), jnp.float32),
            pltpu.VMEM((row_count, width), jnp.bfloat16),
        ],
        compiler_params=grant(returned, norm_gain),
        name="finish",
    )(
        me_scalar,
        places,
        *gates,
        returned.reshape(device_count * capacity, H, head_width),
        norm_gain[None, :],
    )


def solution(mesh):
    return jax.shard_map(
        shards,
        mesh=mesh,
        in_specs=(
            P(AXES, None),
            P(AXES, None),
            P(AXES),
            P("users", None),
            P(),
            P("users", None),
            P("users", "ctx", None),
            P("users", "ctx", None),
            P("users"),
            P("users", "ctx"),
            P(),
            P(),
        ),
        out_specs=P(AXES, None),
        check_vma=False,
    )
```

```python
import functools

import jax
import jax.numpy as jnp
import numpy as np
from jax import lax
from jax.experimental import pallas as pl
from jax.experimental.pallas import tpu as pltpu
from jax.sharding import PartitionSpec as P

H = 8
AXES = ("users", "ctx")
NORM_EPSILON = 1e-05
DEAD = -1e30
VMEM = pltpu.MemorySpace.VMEM
SMEM = pltpu.MemorySpace.SMEM


def round_up(value, step):
    return -(-value // step) * step


def seat(inner, context_count):
    return lax.axis_index("users") % inner * context_count + lax.axis_index("ctx")


def grant(*arrays):
    held = sum(int(np.prod(a.shape)) * a.dtype.itemsize for a in arrays)
    return pltpu.CompilerParams(vmem_limit_bytes=min(60 << 20, 2 * held + (6 << 20)))


def pick_columns(inner, context_count, head_width, context, matrix_ref, columns_ref, skip=0):
    owner_count, _, picked = columns_ref.shape
    blocks = picked // head_width
    width = matrix_ref.shape[1] // (blocks + skip)
    for turn in range(inner):
        for block in range(blocks):
            start = (skip + block) * width + (turn * context_count + context) * head_width
            piece = matrix_ref[:, pl.ds(pl.multiple_of(start, head_width), head_width)]
            for first in range(0, owner_count, inner):
                lanes = slice(block * head_width, (block + 1) * head_width)
                columns_ref[first + turn, :, lanes] = piece


def prepare_kernel(
    inner,
    context_count,
    events_ref,
    owner_ref,
    bucket_ref,
    matrix_ref,
    packed_ref,
    columns_ref,
):
    rows, width = events_ref.shape
    head_width = packed_ref.shape[1] - width
    across = owner_ref[...].astype(jnp.float32)
    owners = jnp.broadcast_to(across, (head_width, rows)).T
    lane = lax.broadcasted_iota(jnp.int32, (rows, rows), 1)
    line = lax.broadcasted_iota(jnp.int32, (rows, rows), 0)
    earlier = (across == owners[:, :1]) & (lane < line)
    ranking = jnp.sum(jnp.where(earlier, 1.0, 0.0), axis=1, keepdims=True)
    buckets = jnp.broadcast_to(bucket_ref[...].astype(jnp.float32), (head_width, rows)).T
    lanes = lax.broadcasted_iota(jnp.int32, (rows, head_width), 1)
    meta = jnp.where(lanes == 0, owners, jnp.where(lanes == 1, ranking, buckets))
    packed_ref[:, :width] = events_ref[...]
    packed_ref[:, width:] = jnp.where(lanes < 3, meta, 0.0).astype(jnp.bfloat16)
    context = lax.axis_index("ctx")
    pick_columns(inner, context_count, head_width, context, matrix_ref, columns_ref)


def spread_columns_kernel(
    inner, context_count, head_width, matrix_ref, columns_ref, *refs
):
    context, user = lax.axis_index("ctx"), lax.axis_index("users")
    pick_columns(inner, context_count, head_width, context, matrix_ref, columns_ref, skip=1)
    half = len(refs) // 2
    for turn in range(half):
        for own, ref in ((user, refs[turn]), (user ^ 1, refs[half + turn])):
            seat = (own & (inner - 1)) ^ (2 * turn & (inner - 1))
            start = (seat * context_count + context) * head_width
            ref[...] = matrix_ref[:, pl.ds(pl.multiple_of(start, head_width), head_width)]


def pair_kernel(*refs):
    count = len(refs) // 3
    rows = refs[0].shape[0]
    mine = lax.axis_index("users") & 1
    for turn in range(count):
        out_ref = refs[2 * count + turn]
        out_ref[pl.ds(pl.multiple_of(mine * rows, rows), rows), :] = refs[turn][...]
        out_ref[pl.ds(pl.multiple_of((1 - mine) * rows, rows), rows), :] = refs[count + turn][...]


def gate_kernel(inner, context_count, crossed_ref, *refs):
    head_count = H
    pieces = refs[: -head_count - 3]
    outs = refs[-head_count - 3 : -3]
    rows_ref, weights_ref, sem = refs[-3:]
    copy = pltpu.make_async_copy(crossed_ref, rows_ref, sem)
    copy.start()
    me, pair = seat(inner, context_count), lax.axis_index("users") >> 1
    depth = pieces[0].shape[0]
    for far, piece in enumerate(pieces):
        weights_ref[pl.ds(pl.multiple_of((pair ^ far) * depth, depth), depth), :] = piece[...]
    copy.wait()
    weights = weights_ref[...]
    rows = outs[0].shape[0]
    for mask in range(head_count):
        source = pl.ds(pl.multiple_of((me ^ mask) * rows, rows), rows)
        half = 0.5 * jnp.dot(rows_ref[source, :], weights, preferred_element_type=jnp.float32)
        outs[mask][...] = (half * (1.0 + jnp.tanh(half))).astype(jnp.bfloat16)


def cross_kernel(inner, context_count, *refs):
    head_count = H
    pieces = refs[:head_count]
    matrix_ref, bias_ref, crossed_ref, meta_ref = refs[head_count:]
    me = seat(inner, context_count)
    rows = pieces[0].shape[0]
    width = bias_ref.shape[1]
    head_width = width // head_count
    columns = pl.ds(pl.multiple_of(me * head_width, head_width), head_width)
    matrix = matrix_ref[...]
    bias = bias_ref[:, columns]
    for mask in range(head_count):
        piece = pieces[mask]
        target = pl.ds(pl.multiple_of((me ^ mask) * rows, rows), rows)
        crossing = jnp.dot(piece[:, :width], matrix, preferred_element_type=jnp.float32)
        source = piece[:, columns].astype(jnp.float32)
        crossed_ref[target, :] = (source * (crossing + bias) + source).astype(jnp.bfloat16)
        meta_ref[target, :] = piece[:, width:]


def project_kernel(inner, context_count, slot_stride, kv_slots, chunk_users, *refs):
    head_count = H
    pieces = refs[:head_count]
    matrix_ref, meta_ref, base_ref = refs[head_count : head_count + 3]
    token_ref, far_rows_ref, out_ref, rows_ref, send_ref, sems = refs[head_count + 3 :]
    token_ref[...] = jnp.zeros_like(token_ref)
    me = seat(inner, context_count)
    head_width = pieces[0].shape[1]
    for mask in range(head_count):
        columns = pl.ds(pl.multiple_of((me ^ mask) * head_width, head_width), head_width)
        rows_ref[:, columns] = pieces[mask][...]
    copy = pltpu.make_async_copy(rows_ref, far_rows_ref, sems.at[0])
    copy.start()
    started = [copy]
    meta = meta_ref[...]
    turned = meta.astype(jnp.float32).T
    owner = turned[0:1, :].astype(jnp.int32)
    rank = turned[1:2, :].astype(jnp.int32)
    slot_of_row = owner * slot_stride + rank + base_ref[...]
    labels = jnp.broadcast_to(meta[:, 2:3].astype(jnp.float32), meta.shape).astype(jnp.bfloat16)
    half = 0.5 * jnp.dot(rows_ref[...], matrix_ref[...], preferred_element_type=jnp.float32)
    activated = (half * (1.0 + jnp.tanh(half))).astype(jnp.bfloat16)
    carried = jnp.concatenate([labels, activated], axis=1)
    user_count = send_ref.shape[0] // context_count
    chunk = chunk_users * slot_stride
    lane = lax.broadcasted_iota(jnp.int32, (8, head_width), 1)
    for turn, first in enumerate(range(0, user_count, chunk_users)):
        slots = lax.broadcasted_iota(jnp.int32, (chunk, slot_of_row.shape[1]), 0)
        picked = (slots + first * slot_stride == slot_of_row).astype(jnp.float32)
        placed = jnp.dot(
            picked.astype(jnp.bfloat16), carried, preferred_element_type=jnp.float32
        )
        for user in range(chunk_users):
            low = user * slot_stride
            queries = placed[low : low + slot_stride, 2 * head_width : 3 * head_width]
            queries = queries.astype(jnp.bfloat16)
            for context in range(context_count):
                target = (first + user) * context_count + context
                start = low + context * kv_slots
                part = placed[start : start + kv_slots]
                send_ref[target, 0:slot_stride, :] = queries
                at = slot_stride
                send_ref[target, at : at + kv_slots, :] = part[:, 3 * head_width :].astype(
                    jnp.bfloat16
                )
                at += kv_slots
                send_ref[target, at : at + kv_slots, :] = part[
                    :, head_width : 2 * head_width
                ].astype(jnp.bfloat16)
                at += kv_slots
                note = part[0:8, :head_width]
                for tile in range(1, kv_slots // 8):
                    note = jnp.where(lane == tile, part[tile * 8 : tile * 8 + 8, :head_width], note)
                send_ref[target, at : at + 8, :] = note.astype(jnp.bfloat16)
        done = pl.ds(first * context_count, chunk_users * context_count)
        copy = pltpu.make_async_copy(send_ref.at[done], out_ref.at[done], sems.at[turn + 1])
        copy.start()
        started.append(copy)
    for copy in started:
        copy.wait()


def stage_kernel(
    capacity,
    length_ref,
    after_ref,
    far_ref,
    bucket_ref,
    time_bias_ref,
    key_order_ref,
    query_order_ref,
    near_ref,
    cache_bias_ref,
    near_time_bias_ref,
    near_key_order_ref,
    near_query_order_ref,
    sem,
):
    copy = pltpu.make_async_copy(far_ref, near_ref, sem)
    copy.start()
    table = time_bias_ref[...]
    shape = (table.shape[1], bucket_ref.shape[1])
    levels = lax.broadcasted_iota(jnp.int32, shape, 0)
    picked = jnp.where(levels == bucket_ref[...], 1.0, 0.0)
    bias = jnp.dot(
        table, picked, precision=lax.Precision.HIGHEST, preferred_element_type=jnp.float32
    )
    positions = lax.broadcasted_iota(jnp.int32, bias.shape, 1)
    context = lax.axis_index("ctx")
    live = length_ref[0] - context * bias.shape[1]
    cache_bias_ref[...] = jnp.where(positions < live, 0.5 * bias, DEAD)
    near_time_bias_ref[...] = table
    near_key_order_ref[...] = key_order_ref[...] + context * capacity
    near_query_order_ref[...] = query_order_ref[...]
    copy.wait()


def attend_kernel(
    slot_stride,
    kv_slots,
    block_groups,
    half_scale,
    recv_ref,
    keys_ref,
    far_values_ref,
    cache_bias_ref,
    time_bias_ref,
    key_order_ref,
    query_order_ref,
    out_ref,
    summed_ref,
    values_ref,
    weights_ref,
    sem,
):
    copy = pltpu.make_async_copy(far_values_ref, values_ref, sem)
    copy.start()
    group_count, head_count, _, head_width = recv_ref.shape
    context_count = slot_stride // kv_slots
    inner = head_count // context_count
    capacity = out_ref.shape[1] // head_count
    block_rows = block_groups * slot_stride
    key_count = group_count * kv_slots
    nt = (((1,), (1,)), ((), ()))
    tn = (((0,), (0,)), ((), ()))

    def weigh(first, head):
        columns = slice(head * head_width, (head + 1) * head_width)
        queries = recv_ref[pl.ds(first, block_groups), head, 0:slot_stride, :]
        queries = queries.reshape(block_rows, head_width)
        scores = lax.dot_general(
            queries, keys_ref[:, columns], nt, preferred_element_type=jnp.float32
        )
        half = scores * half_scale + cache_bias_ref[head : head + 1, :]
        weights_ref[head] = (half * (1.0 + jnp.tanh(half))).astype(jnp.bfloat16)

    def gather(block, first, head):
        columns = slice(head * head_width, (head + 1) * head_width)
        queries = recv_ref[pl.ds(first, block_groups), head, 0:slot_stride, :]
        queries = queries.reshape(block_rows, head_width)
        summed = jnp.dot(
            weights_ref[head], values_ref[:, columns], preferred_element_type=jnp.float32
        )
        at = slot_stride
        new_keys = recv_ref[:, head, at : at + kv_slots, :].reshape(key_count, head_width)
        at += kv_slots
        new_values = recv_ref[:, head, at : at + kv_slots, :].reshape(key_count, head_width)
        at += kv_slots
        notes = recv_ref[:, head, at : at + 8, :].astype(jnp.float32)
        buckets = jnp.concatenate(
            [notes[g, :, t : t + 1] for g in range(group_count) for t in range(kv_slots // 8)],
            axis=0,
        ).astype(jnp.int32)
        table = time_bias_ref[head : head + 1, :]
        levels = lax.broadcasted_iota(jnp.int32, (key_count, table.shape[1]), 1)
        new_bias = jnp.sum(jnp.where(levels == buckets, table, 0.0), axis=1, keepdims=True)
        new_scores = lax.dot_general(new_keys, queries, nt, preferred_element_type=jnp.float32)
        new_half = new_scores * half_scale + 0.5 * new_bias
        new_weights = jnp.where(
            key_order_ref[...] <= query_order_ref[pl.ds(block, 1), :],
            new_half * (1.0 + jnp.tanh(new_half)),
            0.0,
        ).astype(jnp.bfloat16)
        summed = summed + lax.dot_general(
            new_weights, new_values, tn, preferred_element_type=jnp.float32
        )
        summed_ref[pl.ds(head, block_rows, stride=head_count), :] = summed

    def one_block(block, waits):
        first = block * block_groups
        lag = head_count // 2
        for head in range(head_count + lag):
            if head < head_count:
                weigh(first, head)
            if waits and head == lag:
                copy.wait()
            if head >= lag:
                gather(block, first, head - lag)
        for group in range(block_groups):
            for context in range(context_count):
                for turn in range(inner):
                    slot = (group * context_count + context) * kv_slots + turn * capacity
                    rows = slice(slot * head_count, (slot + capacity) * head_count)
                    target = (first + group) * head_count + turn * context_count + context
                    out_ref[target] = summed_ref[rows, :].astype(jnp.bfloat16)

    block_count = group_count // block_groups
    if block_count == 1:
        one_block(0, True)
    else:
        copy.wait()

        def step(block, carry):
            one_block(block, False)
            return carry

        lax.fori_loop(0, block_count, step, 0)


def finish_kernel(inner, context_count, place_ref, *refs):
    head_count = H
    gates = refs[:head_count]
    returned_ref, gain_ref, out_ref, tall_ref, gate_ref = refs[head_count:]
    me = seat(inner, context_count)
    rows, width = out_ref.shape
    head_width = width // head_count
    for mask in range(head_count):
        columns = pl.ds(pl.multiple_of((me ^ mask) * head_width, head_width), head_width)
        gate_ref[:, columns] = gates[mask][...]
    for row in range(rows):
        total = returned_ref[place_ref[row, 0]].astype(jnp.float32)
        for context in range(1, place_ref.shape[1]):
            total = total + returned_ref[place_ref[row, context]].astype(jnp.float32)
        tall_ref[row * head_count : (row + 1) * head_count, :] = total
    attended = jnp.concatenate(
        [tall_ref[pl.ds(head, rows, stride=head_count), :] for head in range(head_count)], axis=1
    )
    center = jnp.mean(attended, axis=1, keepdims=True)
    moved = attended - center
    spread = jnp.mean(jnp.square(moved), axis=1, keepdims=True)
    normed = moved * lax.rsqrt(spread + NORM_EPSILON)
    out_ref[...] = (normed * gain_ref[...] * gate_ref[...].astype(jnp.float32)).astype(jnp.bfloat16)


def shards(
    events,
    owner_id,
    event_bucket,
    cross_weight,
    cross_bias,
    project_weight,
    cache_keys,
    cache_values,
    cache_length,
    cache_bucket,
    time_bias,
    norm_gain,
):
    row_count, width = events.shape
    head_width = width // H
    owner_count = lax.axis_size("users")
    context_count = lax.axis_size("ctx")
    device_count = owner_count * context_count
    inner = H // context_count
    group_count = owner_count // inner
    capacity = max(2, (3 * row_count + 2 * owner_count - 1) // (2 * owner_count))
    kv_slots = round_up(inner * capacity, 8)
    slot_stride = context_count * kv_slots
    cache_rows = cache_keys.shape[1]
    bucket_count = time_bias.shape[0]
    group_rows = H * row_count
    core = context_count if inner > 1 else 0
    blocks = project_weight.shape[1] // width

    def swap(block, mask):
        pairs = [(d, d // H * H + (d % H ^ mask)) for d in range(device_count)]
        return lax.ppermute(block, AXES, pairs)

    def spread(block):
        pieces = [block] + [None] * (H - 1)
        for mask in range(1, H):
            if not mask & core:
                pieces[mask] = swap(block, mask)
        for mask in range(H):
            if mask & core:
                pieces[mask] = swap(pieces[mask ^ core], core)
        return pieces

    owners = owner_id[:, 0]
    positions = jnp.arange(row_count, dtype=jnp.int32)
    earlier = (owners[None, :] == owners[:, None]) & (positions[None, :] < positions[:, None])
    ranking = jnp.sum(earlier.astype(jnp.int32), axis=1)
    vmem_spec = pl.BlockSpec(memory_space=VMEM)
    smem_spec = pl.BlockSpec(memory_space=SMEM)
    hbm_spec = pl.BlockSpec(memory_space=pltpu.MemorySpace.HBM)
    packed_shape = jax.ShapeDtypeStruct((row_count, width + head_width), jnp.bfloat16)
    matrix_rows = cross_weight.shape[0]
    cross_shape = jax.ShapeDtypeStruct((owner_count, matrix_rows, head_width), jnp.bfloat16)
    packed, cross_columns = pl.pallas_call(
        functools.partial(prepare_kernel, inner, context_count),
        out_shape=(packed_shape, cross_shape),
        in_specs=[vmem_spec] * 4,
        out_specs=(vmem_spec, vmem_spec),
        name="prepare",
    )(events, owner_id.reshape(1, -1), event_bucket[None, :], cross_weight)
    pieces = spread(packed)
    project_shape = jax.ShapeDtypeStruct(
        (owner_count, matrix_rows, (blocks - 1) * head_width), jnp.bfloat16
    )
    gate_kinds = max(1, inner // 2)
    gate_shape = jax.ShapeDtypeStruct((matrix_rows, head_width), jnp.bfloat16)
    project_columns, *gate_columns = pl.pallas_call(
        functools.partial(spread_columns_kernel, inner, context_count, head_width),
        out_shape=[project_shape] + [gate_shape] * (2 * gate_kinds),
        in_specs=[vmem_spec],
        out_specs=[vmem_spec] * (1 + 2 * gate_kinds),
        compiler_params=grant(project_shape),
        name="columns",
    )(project_weight)

    cross_columns = lax.all_to_all(cross_columns, "users", split_axis=0, concat_axis=0, tiled=True)
    project_columns = lax.all_to_all(
        project_columns, "users", split_axis=0, concat_axis=0, tiled=True
    )
    project_columns = project_columns.reshape(width, (blocks - 1) * head_width)
    cross_columns = cross_columns.reshape(width, head_width)

    def trade(block, mask):
        pairs = [
            (u * context_count + c, (u ^ mask) * context_count + c)
            for u in range(owner_count)
            for c in range(context_count)
        ]
        return lax.ppermute(block, AXES, pairs)

    gate_other = [trade(block, 1) for block in gate_columns[gate_kinds:]]
    gate_pairs = pl.pallas_call(
        pair_kernel,
        out_shape=[jax.ShapeDtypeStruct((2 * matrix_rows, head_width), jnp.bfloat16)]
        * gate_kinds,
        in_specs=[vmem_spec] * (2 * gate_kinds),
        out_specs=[vmem_spec] * gate_kinds,
        compiler_params=grant(project_shape),
        name="pair",
    )(*gate_columns[:gate_kinds], *gate_other)
    gate_pieces = [gate_pairs[0]] + [
        trade(gate_pairs[mask // 2 % gate_kinds], mask) for mask in range(2, owner_count, 2)
    ]

    crossed, group_meta = pl.pallas_call(
        functools.partial(cross_kernel, inner, context_count),
        out_shape=(
            jax.ShapeDtypeStruct((group_rows, head_width), jnp.bfloat16),
            jax.ShapeDtypeStruct((group_rows, head_width), jnp.bfloat16),
        ),
        in_specs=[vmem_spec] * (H + 2),
        out_specs=(vmem_spec, vmem_spec),
        compiler_params=grant(*pieces, cross_columns),
        name="cross",
    )(*pieces, cross_columns, cross_bias[None, :])
    crossed_pieces = spread(crossed)

    shard = np.arange(group_rows) // row_count
    base = ((shard % context_count) * kv_slots + (shard // context_count) * capacity)[None, :]
    message_rows = slot_stride + 2 * kv_slots + 8
    chunk_users = max(1, min(owner_count, 512 // slot_stride))
    while owner_count % chunk_users:
        chunk_users -= 1
    messages = jax.ShapeDtypeStruct((device_count, message_rows, head_width), jnp.bfloat16)
    token, far_rows, outgoing = pl.pallas_call(
        functools.partial(project_kernel, inner, context_count, slot_stride, kv_slots, chunk_users),
        out_shape=[
            jax.ShapeDtypeStruct((8, head_width), jnp.float32),
            pltpu.MemorySpace.HBM((group_rows, width), jnp.bfloat16),
            messages,
        ],
        in_specs=[vmem_spec] * (H + 3),
        out_specs=[vmem_spec] + [hbm_spec] * 2,
        scratch_shapes=[
            pltpu.VMEM((group_rows, width), jnp.bfloat16),
            pltpu.VMEM(messages.shape, messages.dtype),
            pltpu.SemaphoreType.DMA((owner_count // chunk_users + 1,)),
        ],
        compiler_params=grant(*crossed_pieces, project_columns, messages, messages),
        name="project",
    )(*crossed_pieces, project_columns, group_meta, jnp.asarray(base, jnp.int32))
    gates = pl.pallas_call(
        functools.partial(gate_kernel, inner, context_count),
        out_shape=[jax.ShapeDtypeStruct((row_count, head_width), jnp.bfloat16)] * H,
        in_specs=[hbm_spec] + [vmem_spec] * len(gate_pieces),
        out_specs=[vmem_spec] * H,
        scratch_shapes=[
            pltpu.VMEM((group_rows, width), jnp.bfloat16),
            pltpu.VMEM((width, head_width), jnp.bfloat16),
            pltpu.SemaphoreType.DMA(()),
        ],
        compiler_params=grant(far_rows),
        name="gate",
    )(
        pltpu.with_memory_space_constraint(far_rows, pltpu.MemorySpace.HBM),
        *gate_pieces,
    )
    gates = [gates[0]] + [swap(gates[mask], mask) for mask in range(1, H)]

    arrived = lax.all_to_all(outgoing, AXES, split_axis=0, concat_axis=0, tiled=True)
    arrived = arrived.reshape(group_count, H, message_rows, head_width)

    def order_of(group, context, rest):
        member = rest // capacity * context_count + context
        return (group * H + member) * capacity + rest % capacity

    slots = np.arange(group_count * slot_stride)
    query_order = order_of(slots // slot_stride, slots % slot_stride // kv_slots, slots % kv_slots)
    slots = np.arange(group_count * kv_slots)
    key_order = jnp.asarray(order_of(slots // kv_slots, 0, slots % kv_slots), jnp.int32)
    block_groups = max(1, min(group_count, 256 // slot_stride))
    while group_count % block_groups:
        block_groups -= 1
    block_rows = block_groups * slot_stride
    query_order = jnp.asarray(query_order, jnp.int32).reshape(-1, block_rows)

    def far(cache):
        return pltpu.with_memory_space_constraint(cache[0], pltpu.MemorySpace.HBM)

    near = pl.pallas_call(
        functools.partial(stage_kernel, capacity),
        out_shape=(
            jax.ShapeDtypeStruct(cache_keys.shape[1:], cache_keys.dtype),
            jax.ShapeDtypeStruct((H, cache_rows), jnp.float32),
            jax.ShapeDtypeStruct((H, bucket_count), jnp.float32),
            jax.ShapeDtypeStruct((group_count * kv_slots, 1), jnp.int32),
            jax.ShapeDtypeStruct(query_order.shape, jnp.int32),
        ),
        in_specs=[smem_spec, vmem_spec, hbm_spec] + [vmem_spec] * 4,
        out_specs=[vmem_spec] * 5,
        scratch_shapes=[pltpu.SemaphoreType.DMA(())],
        compiler_params=grant(cache_keys),
        name="stage",
    )(
        cache_length,
        token,
        far(cache_keys),
        cache_bucket,
        time_bias.T,
        key_order[:, None],
        query_order,
    )

    partials = pl.pallas_call(
        functools.partial(
            attend_kernel, slot_stride, kv_slots, block_groups, 0.5 * head_width**-0.5
        ),
        out_shape=jax.ShapeDtypeStruct((device_count, capacity * H, head_width), jnp.bfloat16),
        in_specs=[vmem_spec] * 2 + [hbm_spec] + [vmem_spec] * 4,
        out_specs=vmem_spec,
        scratch_shapes=[
            pltpu.VMEM((block_rows * H, head_width), jnp.float32),
            pltpu.VMEM(cache_values.shape[1:], cache_values.dtype),
            pltpu.VMEM((H, block_rows, cache_rows), jnp.bfloat16),
            pltpu.SemaphoreType.DMA(()),
        ],
        compiler_params=grant(arrived, cache_keys, cache_values, query_order),
        name="attend",
    )(arrived, near[0], far(cache_values), *near[1:])

    returned = lax.all_to_all(partials, AXES, split_axis=0, concat_axis=0, tiled=True)
    contexts = jnp.arange(context_count, dtype=jnp.int32)[None, :]
    places = (owners[:, None] * context_count + contexts) * capacity + ranking[:, None]
    return pl.pallas_call(
        functools.partial(finish_kernel, inner, context_count),
        out_shape=jax.ShapeDtypeStruct((row_count, width), jnp.bfloat16),
        in_specs=[smem_spec] + [vmem_spec] * (H + 2),
        out_specs=vmem_spec,
        scratch_shapes=[
            pltpu.VMEM((row_count * H, head_width), jnp.float32),
            pltpu.VMEM((row_count, width), jnp.bfloat16),
        ],
        compiler_params=grant(returned, norm_gain),
        name="finish",
    )(
        places,
        *gates,
        returned.reshape(device_count * capacity, H, head_width),
        norm_gain[None, :],
    )


def solution(mesh):
    return jax.shard_map(
        shards,
        mesh=mesh,
        in_specs=(
            P(AXES, None),
            P(AXES, None),
            P(AXES),
            P("users", None),
            P(),
            P("users", None),
            P("users", "ctx", None),
            P("users", "ctx", None),
            P("users"),
            P("users", "ctx"),
            P(),
            P(),
        ),
        out_specs=P(AXES, None),
        check_vma=False,
    )
```

```python
import functools

import jax
import jax.numpy as jnp
import numpy as np
from jax import lax
from jax.experimental import pallas as pl
from jax.experimental.pallas import tpu as pltpu
from jax.sharding import PartitionSpec as P

H = 8
AXES = ("users", "ctx")
NORM_EPSILON = 1e-05
DEAD = -1e30
VMEM = pltpu.MemorySpace.VMEM
SMEM = pltpu.MemorySpace.SMEM


def round_up(value, step):
    return -(-value // step) * step


def seat(inner, context_count):
    return lax.axis_index("users") % inner * context_count + lax.axis_index("ctx")


def grant(*arrays):
    held = sum(int(np.prod(a.shape)) * a.dtype.itemsize for a in arrays)
    return pltpu.CompilerParams(vmem_limit_bytes=min(60 << 20, 2 * held + (6 << 20)))


def pick_columns(inner, context_count, head_width, context, matrix_ref, columns_ref, skip=0):
    owner_count, _, picked = columns_ref.shape
    blocks = picked // head_width
    width = matrix_ref.shape[1] // (blocks + skip)
    for turn in range(inner):
        for block in range(blocks):
            start = (skip + block) * width + (turn * context_count + context) * head_width
            piece = matrix_ref[:, pl.ds(pl.multiple_of(start, head_width), head_width)]
            for first in range(0, owner_count, inner):
                lanes = slice(block * head_width, (block + 1) * head_width)
                columns_ref[first + turn, :, lanes] = piece


def prepare_kernel(events_ref, owner_ref, bucket_ref, packed_ref):
    rows, width = events_ref.shape
    head_width = packed_ref.shape[1] - width
    across = owner_ref[...].astype(jnp.float32)
    owners = jnp.broadcast_to(across, (head_width, rows)).T
    lane = lax.broadcasted_iota(jnp.int32, (rows, rows), 1)
    line = lax.broadcasted_iota(jnp.int32, (rows, rows), 0)
    earlier = (across == owners[:, :1]) & (lane < line)
    ranking = jnp.sum(jnp.where(earlier, 1.0, 0.0), axis=1, keepdims=True)
    buckets = jnp.broadcast_to(bucket_ref[...].astype(jnp.float32), (head_width, rows)).T
    lanes = lax.broadcasted_iota(jnp.int32, (rows, head_width), 1)
    meta = jnp.where(lanes == 0, owners, jnp.where(lanes == 1, ranking, buckets))
    packed_ref[:, :width] = events_ref[...]
    packed_ref[:, width:] = jnp.where(lanes < 3, meta, 0.0).astype(jnp.bfloat16)


def cross_columns_kernel(inner, context_count, head_width, matrix_ref, columns_ref):
    context = lax.axis_index("ctx")
    pick_columns(inner, context_count, head_width, context, matrix_ref, columns_ref)


def spread_columns_kernel(
    inner, context_count, head_width, matrix_ref, columns_ref, *refs
):
    context, user = lax.axis_index("ctx"), lax.axis_index("users")
    pick_columns(inner, context_count, head_width, context, matrix_ref, columns_ref, skip=1)
    half = len(refs) // 2
    for turn in range(half):
        for own, ref in ((user, refs[turn]), (user ^ 1, refs[half + turn])):
            seat = (own & (inner - 1)) ^ (2 * turn & (inner - 1))
            start = (seat * context_count + context) * head_width
            ref[...] = matrix_ref[:, pl.ds(pl.multiple_of(start, head_width), head_width)]


def pair_kernel(*refs):
    count = len(refs) // 3
    rows = refs[0].shape[0]
    mine = lax.axis_index("users") & 1
    for turn in range(count):
        out_ref = refs[2 * count + turn]
        out_ref[pl.ds(pl.multiple_of(mine * rows, rows), rows), :] = refs[turn][...]
        out_ref[pl.ds(pl.multiple_of((1 - mine) * rows, rows), rows), :] = refs[count + turn][...]


def gate_kernel(inner, context_count, crossed_ref, *refs):
    head_count = H
    pieces = refs[: -head_count - 3]
    outs = refs[-head_count - 3 : -3]
    rows_ref, weights_ref, sem = refs[-3:]
    copy = pltpu.make_async_copy(crossed_ref, rows_ref, sem)
    copy.start()
    me, pair = seat(inner, context_count), lax.axis_index("users") >> 1
    depth = pieces[0].shape[0]
    for far, piece in enumerate(pieces):
        weights_ref[pl.ds(pl.multiple_of((pair ^ far) * depth, depth), depth), :] = piece[...]
    copy.wait()
    weights = weights_ref[...]
    rows = outs[0].shape[0]
    for mask in range(head_count):
        source = pl.ds(pl.multiple_of((me ^ mask) * rows, rows), rows)
        half = 0.5 * jnp.dot(rows_ref[source, :], weights, preferred_element_type=jnp.float32)
        outs[mask][...] = (half * (1.0 + jnp.tanh(half))).astype(jnp.bfloat16)


def cross_kernel(inner, context_count, *refs):
    head_count = H
    pieces = refs[:head_count]
    matrix_ref, bias_ref, crossed_ref, turned_ref, meta_ref = refs[head_count:]
    me = seat(inner, context_count)
    rows = pieces[0].shape[0]
    width = bias_ref.shape[1]
    head_width = width // head_count
    columns = pl.ds(pl.multiple_of(me * head_width, head_width), head_width)
    matrix = matrix_ref[...]
    bias = bias_ref[:, columns]
    for mask in range(head_count):
        piece = pieces[mask]
        target = pl.ds(pl.multiple_of((me ^ mask) * rows, rows), rows)
        crossing = jnp.dot(piece[:, :width], matrix, preferred_element_type=jnp.float32)
        source = piece[:, columns].astype(jnp.float32)
        crossed_ref[target, :] = (source * (crossing + bias) + source).astype(jnp.bfloat16)
        meta_ref[target, :] = piece[:, width:].astype(jnp.float32)
    turned_ref[...] = meta_ref[...].T[: turned_ref.shape[0], :]


def project_kernel(inner, context_count, slot_stride, kv_slots, chunk_users, *refs):
    head_count = H
    pieces = refs[:head_count]
    matrix_ref, meta_ref, base_ref = refs[head_count : head_count + 3]
    token_ref, far_rows_ref, out_ref, rows_ref, send_ref, sems = refs[head_count + 3 :]
    token_ref[...] = jnp.zeros_like(token_ref)
    me = seat(inner, context_count)
    head_width = pieces[0].shape[1]
    for mask in range(head_count):
        columns = pl.ds(pl.multiple_of((me ^ mask) * head_width, head_width), head_width)
        rows_ref[:, columns] = pieces[mask][...]
    copy = pltpu.make_async_copy(rows_ref, far_rows_ref, sems.at[0])
    copy.start()
    started = [copy]
    owner = meta_ref[0:1, :].astype(jnp.int32)
    rank = meta_ref[1:2, :].astype(jnp.int32)
    slot_of_row = owner * slot_stride + rank + base_ref[...]
    half = 0.5 * jnp.dot(rows_ref[...], matrix_ref[...], preferred_element_type=jnp.float32)
    activated = (half * (1.0 + jnp.tanh(half))).astype(jnp.bfloat16)
    user_count = send_ref.shape[0] // context_count
    chunk = chunk_users * slot_stride
    for turn, first in enumerate(range(0, user_count, chunk_users)):
        slots = lax.broadcasted_iota(jnp.int32, (chunk, slot_of_row.shape[1]), 0)
        picked = (slots + first * slot_stride == slot_of_row).astype(jnp.float32)
        placed = jnp.dot(
            picked.astype(jnp.bfloat16), activated, preferred_element_type=jnp.float32
        )
        for user in range(chunk_users):
            low = user * slot_stride
            queries = placed[low : low + slot_stride, head_width : 2 * head_width]
            queries = queries.astype(jnp.bfloat16)
            for context in range(context_count):
                target = (first + user) * context_count + context
                start = low + context * kv_slots
                part = placed[start : start + kv_slots]
                send_ref[target, 0:slot_stride, :] = queries
                at = slot_stride
                send_ref[target, at : at + kv_slots, :] = part[:, 2 * head_width :].astype(
                    jnp.bfloat16
                )
                at += kv_slots
                send_ref[target, at : at + kv_slots, :] = part[:, :head_width].astype(
                    jnp.bfloat16
                )
        done = pl.ds(first * context_count, chunk_users * context_count)
        copy = pltpu.make_async_copy(send_ref.at[done], out_ref.at[done], sems.at[turn + 1])
        copy.start()
        started.append(copy)
    for copy in started:
        copy.wait()


def stage_kernel(inner, capacity, kv_slots, length_ref, after_ref, far_ref, *refs):
    bucket_ref, time_bias_ref, key_order_ref, query_order_ref, base_ref = refs[:5]
    metas = refs[5:-7]
    near_ref, cache_bias_ref, new_bias_ref, near_key_order_ref, near_query_order_ref = refs[-7:-2]
    found_ref, sem = refs[-2:]
    copy = pltpu.make_async_copy(far_ref, near_ref, sem)
    copy.start()
    user, context = lax.axis_index("users"), lax.axis_index("ctx")
    table = time_bias_ref[...]
    shape = (table.shape[1], bucket_ref.shape[1])
    levels = lax.broadcasted_iota(jnp.int32, shape, 0)
    picked = jnp.where(levels == bucket_ref[...], 1.0, 0.0)
    bias = jnp.dot(
        table, picked, precision=lax.Precision.HIGHEST, preferred_element_type=jnp.float32
    )
    positions = lax.broadcasted_iota(jnp.int32, bias.shape, 1)
    live = length_ref[0] - context * bias.shape[1]
    cache_bias_ref[...] = jnp.where(positions < live, 0.5 * bias, DEAD)
    group = user // inner
    for mask, meta_ref in enumerate(metas):
        place = meta_ref[1:2, :].astype(jnp.int32) + base_ref[...] - context * kv_slots
        place = jnp.where(meta_ref[0:1, :].astype(jnp.int32) == user, place, -1)
        slots = lax.broadcasted_iota(jnp.int32, (kv_slots, place.shape[1]), 0)
        found = jnp.sum(jnp.where(slots == place, meta_ref[2:3, :], 0.0), axis=1, keepdims=True)
        target = pl.ds(pl.multiple_of((group ^ mask) * kv_slots, 8), kv_slots)
        found_ref[target, :] = jnp.broadcast_to(found, (kv_slots, found_ref.shape[1]))
    levels = lax.broadcasted_iota(jnp.int32, (found_ref.shape[0], table.shape[1]), 1)
    hits = jnp.where(levels == found_ref[:, 0:1].astype(jnp.int32), 1.0, 0.0)
    new_bias_ref[...] = 0.5 * lax.dot_general(
        hits,
        table,
        (((1,), (1,)), ((), ())),
        precision=lax.Precision.HIGHEST,
        preferred_element_type=jnp.float32,
    )
    near_key_order_ref[...] = key_order_ref[...] + context * capacity
    near_query_order_ref[...] = query_order_ref[...]
    copy.wait()


def attend_kernel(
    slot_stride,
    kv_slots,
    block_groups,
    half_scale,
    recv_ref,
    keys_ref,
    far_values_ref,
    cache_bias_ref,
    new_bias_ref,
    key_order_ref,
    query_order_ref,
    out_ref,
    summed_ref,
    values_ref,
    weights_ref,
    sem,
):
    copy = pltpu.make_async_copy(far_values_ref, values_ref, sem)
    copy.start()
    group_count, head_count, _, head_width = recv_ref.shape
    context_count = slot_stride // kv_slots
    inner = head_count // context_count
    capacity = out_ref.shape[1] // head_count
    block_rows = block_groups * slot_stride
    key_count = group_count * kv_slots
    nt = (((1,), (1,)), ((), ()))
    tn = (((0,), (0,)), ((), ()))

    def weigh(first, head):
        columns = slice(head * head_width, (head + 1) * head_width)
        queries = recv_ref[pl.ds(first, block_groups), head, 0:slot_stride, :]
        queries = queries.reshape(block_rows, head_width)
        scores = lax.dot_general(
            queries, keys_ref[:, columns], nt, preferred_element_type=jnp.float32
        )
        half = scores * half_scale + cache_bias_ref[head : head + 1, :]
        weights_ref[head] = (half * (1.0 + jnp.tanh(half))).astype(jnp.bfloat16)

    def gather(block, first, head):
        columns = slice(head * head_width, (head + 1) * head_width)
        queries = recv_ref[pl.ds(first, block_groups), head, 0:slot_stride, :]
        queries = queries.reshape(block_rows, head_width)
        summed = jnp.dot(
            weights_ref[head], values_ref[:, columns], preferred_element_type=jnp.float32
        )
        at = slot_stride
        new_keys = recv_ref[:, head, at : at + kv_slots, :].reshape(key_count, head_width)
        at += kv_slots
        new_values = recv_ref[:, head, at : at + kv_slots, :].reshape(key_count, head_width)
        new_scores = lax.dot_general(new_keys, queries, nt, preferred_element_type=jnp.float32)
        new_half = new_scores * half_scale + new_bias_ref[:, head : head + 1]
        new_weights = jnp.where(
            key_order_ref[...] <= query_order_ref[pl.ds(block, 1), :],
            new_half * (1.0 + jnp.tanh(new_half)),
            0.0,
        ).astype(jnp.bfloat16)
        summed = summed + lax.dot_general(
            new_weights, new_values, tn, preferred_element_type=jnp.float32
        )
        summed_ref[pl.ds(head, block_rows, stride=head_count), :] = summed

    def one_block(block, waits):
        first = block * block_groups
        lag = head_count // 2
        for head in range(head_count + lag):
            if head < head_count:
                weigh(first, head)
            if waits and head == lag:
                copy.wait()
            if head >= lag:
                gather(block, first, head - lag)
        for group in range(block_groups):
            for context in range(context_count):
                for turn in range(inner):
                    slot = (group * context_count + context) * kv_slots + turn * capacity
                    rows = slice(slot * head_count, (slot + capacity) * head_count)
                    target = (first + group) * head_count + turn * context_count + context
                    out_ref[target] = summed_ref[rows, :].astype(jnp.bfloat16)

    block_count = group_count // block_groups
    if block_count == 1:
        one_block(0, True)
    else:
        copy.wait()

        def step(block, carry):
            one_block(block, False)
            return carry

        lax.fori_loop(0, block_count, step, 0)


def finish_kernel(inner, context_count, place_ref, *refs):
    head_count = H
    gates = refs[:head_count]
    returned_ref, gain_ref, out_ref, tall_ref, gate_ref = refs[head_count:]
    me = seat(inner, context_count)
    rows, width = out_ref.shape
    head_width = width // head_count
    for mask in range(head_count):
        columns = pl.ds(pl.multiple_of((me ^ mask) * head_width, head_width), head_width)
        gate_ref[:, columns] = gates[mask][...]
    for row in range(rows):
        total = returned_ref[place_ref[0, row]].astype(jnp.float32)
        for context in range(1, context_count):
            total = total + returned_ref[place_ref[context, row]].astype(jnp.float32)
        tall_ref[row * head_count : (row + 1) * head_count, :] = total
    attended = jnp.concatenate(
        [tall_ref[pl.ds(head, rows, stride=head_count), :] for head in range(head_count)], axis=1
    )
    center = jnp.mean(attended, axis=1, keepdims=True)
    moved = attended - center
    spread = jnp.mean(jnp.square(moved), axis=1, keepdims=True)
    normed = moved * lax.rsqrt(spread + NORM_EPSILON)
    out_ref[...] = (normed * gain_ref[...] * gate_ref[...].astype(jnp.float32)).astype(jnp.bfloat16)


def shards(
    events,
    owner_id,
    event_bucket,
    cross_weight,
    cross_bias,
    project_weight,
    cache_keys,
    cache_values,
    cache_length,
    cache_bucket,
    time_bias,
    norm_gain,
):
    row_count, width = events.shape
    head_width = width // H
    owner_count = lax.axis_size("users")
    context_count = lax.axis_size("ctx")
    device_count = owner_count * context_count
    inner = H // context_count
    group_count = owner_count // inner
    capacity = max(2, (3 * row_count + 2 * owner_count - 1) // (2 * owner_count))
    kv_slots = round_up(inner * capacity, 8)
    slot_stride = context_count * kv_slots
    cache_rows = cache_keys.shape[1]
    group_rows = H * row_count
    core = context_count if inner > 1 else 0
    blocks = project_weight.shape[1] // width

    def swap(block, mask):
        pairs = [(d, d // H * H + (d % H ^ mask)) for d in range(device_count)]
        return lax.ppermute(block, AXES, pairs)

    def spread(block):
        pieces = [block] + [None] * (H - 1)
        for mask in range(1, H):
            if not mask & core:
                pieces[mask] = swap(block, mask)
        for mask in range(H):
            if mask & core:
                pieces[mask] = swap(pieces[mask ^ core], core)
        return pieces

    owners = owner_id[:, 0]
    positions = jnp.arange(row_count, dtype=jnp.int32)
    earlier = (owners[None, :] == owners[:, None]) & (positions[None, :] < positions[:, None])
    ranking = jnp.sum(earlier.astype(jnp.int32), axis=1)
    vmem_spec = pl.BlockSpec(memory_space=VMEM)
    smem_spec = pl.BlockSpec(memory_space=SMEM)
    hbm_spec = pl.BlockSpec(memory_space=pltpu.MemorySpace.HBM)
    packed_shape = jax.ShapeDtypeStruct((row_count, width + head_width), jnp.bfloat16)
    matrix_rows = cross_weight.shape[0]
    cross_shape = jax.ShapeDtypeStruct((owner_count, matrix_rows, head_width), jnp.bfloat16)
    cross_columns = pl.pallas_call(
        functools.partial(cross_columns_kernel, inner, context_count, head_width),
        out_shape=cross_shape,
        in_specs=[vmem_spec],
        out_specs=vmem_spec,
        name="cross_columns",
    )(cross_weight)
    packed = pl.pallas_call(
        prepare_kernel,
        out_shape=packed_shape,
        in_specs=[vmem_spec] * 3,
        out_specs=vmem_spec,
        name="prepare",
    )(events, owner_id.reshape(1, -1), event_bucket[None, :])
    pieces = spread(packed)
    project_shape = jax.ShapeDtypeStruct(
        (owner_count, matrix_rows, (blocks - 1) * head_width), jnp.bfloat16
    )
    gate_kinds = max(1, inner // 2)
    gate_shape = jax.ShapeDtypeStruct((matrix_rows, head_width), jnp.bfloat16)
    project_columns, *gate_columns = pl.pallas_call(
        functools.partial(spread_columns_kernel, inner, context_count, head_width),
        out_shape=[project_shape] + [gate_shape] * (2 * gate_kinds),
        in_specs=[vmem_spec],
        out_specs=[vmem_spec] * (1 + 2 * gate_kinds),
        compiler_params=grant(project_shape),
        name="columns",
    )(project_weight)

    cross_columns = lax.all_to_all(cross_columns, "users", split_axis=0, concat_axis=0, tiled=True)
    project_columns = lax.all_to_all(
        project_columns, "users", split_axis=0, concat_axis=0, tiled=True
    )
    project_columns = project_columns.reshape(width, (blocks - 1) * head_width)
    cross_columns = cross_columns.reshape(width, head_width)

    def trade(block, mask):
        pairs = [
            (u * context_count + c, (u ^ mask) * context_count + c)
            for u in range(owner_count)
            for c in range(context_count)
        ]
        return lax.ppermute(block, AXES, pairs)

    gate_other = [trade(block, 1) for block in gate_columns[gate_kinds:]]
    gate_pairs = pl.pallas_call(
        pair_kernel,
        out_shape=[jax.ShapeDtypeStruct((2 * matrix_rows, head_width), jnp.bfloat16)]
        * gate_kinds,
        in_specs=[vmem_spec] * (2 * gate_kinds),
        out_specs=[vmem_spec] * gate_kinds,
        compiler_params=grant(project_shape),
        name="pair",
    )(*gate_columns[:gate_kinds], *gate_other)
    gate_pieces = [gate_pairs[0]] + [
        trade(gate_pairs[mask // 2 % gate_kinds], mask) for mask in range(2, owner_count, 2)
    ]

    meta_shape = jax.ShapeDtypeStruct((8, group_rows), jnp.float32)
    crossed, group_meta = pl.pallas_call(
        functools.partial(cross_kernel, inner, context_count),
        out_shape=(
            jax.ShapeDtypeStruct((group_rows, head_width), jnp.bfloat16),
            meta_shape,
        ),
        in_specs=[vmem_spec] * (H + 2),
        out_specs=(vmem_spec, vmem_spec),
        scratch_shapes=[pltpu.VMEM((group_rows, head_width), jnp.float32)],
        compiler_params=grant(*pieces, cross_columns),
        name="cross",
    )(*pieces, cross_columns, cross_bias[None, :])
    crossed_pieces = spread(crossed)
    metas = [group_meta]
    for mask in range(1, group_count):
        pairs = [
            (g * H + member, (g ^ mask) * H + member)
            for g in range(group_count)
            for member in range(H)
        ]
        metas.append(lax.ppermute(group_meta, AXES, pairs))

    shard = np.arange(group_rows) // row_count
    base = ((shard % context_count) * kv_slots + (shard // context_count) * capacity)[None, :]
    message_rows = slot_stride + 2 * kv_slots
    base = jnp.asarray(base, jnp.int32)
    chunk_users = max(1, min(owner_count, 256 // slot_stride))
    while owner_count % chunk_users:
        chunk_users -= 1
    messages = jax.ShapeDtypeStruct((device_count, message_rows, head_width), jnp.bfloat16)
    token, far_rows, outgoing = pl.pallas_call(
        functools.partial(project_kernel, inner, context_count, slot_stride, kv_slots, chunk_users),
        out_shape=[
            jax.ShapeDtypeStruct((8, head_width), jnp.float32),
            pltpu.MemorySpace.HBM((group_rows, width), jnp.bfloat16),
            messages,
        ],
        in_specs=[vmem_spec] * (H + 3),
        out_specs=[vmem_spec] + [hbm_spec] * 2,
        scratch_shapes=[
            pltpu.VMEM((group_rows, width), jnp.bfloat16),
            pltpu.VMEM(messages.shape, messages.dtype),
            pltpu.SemaphoreType.DMA((owner_count // chunk_users + 1,)),
        ],
        compiler_params=grant(*crossed_pieces, project_columns, messages, messages),
        name="project",
    )(*crossed_pieces, project_columns, group_meta, base)
    gates = pl.pallas_call(
        functools.partial(gate_kernel, inner, context_count),
        out_shape=[jax.ShapeDtypeStruct((row_count, head_width), jnp.bfloat16)] * H,
        in_specs=[hbm_spec] + [vmem_spec] * len(gate_pieces),
        out_specs=[vmem_spec] * H,
        scratch_shapes=[
            pltpu.VMEM((group_rows, width), jnp.bfloat16),
            pltpu.VMEM((width, head_width), jnp.bfloat16),
            pltpu.SemaphoreType.DMA(()),
        ],
        compiler_params=grant(far_rows),
        name="gate",
    )(
        pltpu.with_memory_space_constraint(far_rows, pltpu.MemorySpace.HBM),
        *gate_pieces,
    )
    gates = [gates[0]] + [swap(gates[mask], mask) for mask in range(1, H)]

    arrived = lax.all_to_all(outgoing, AXES, split_axis=0, concat_axis=0, tiled=True)
    arrived = arrived.reshape(group_count, H, message_rows, head_width)

    def order_of(group, context, rest):
        member = rest // capacity * context_count + context
        return (group * H + member) * capacity + rest % capacity

    slots = np.arange(group_count * slot_stride)
    query_order = order_of(slots // slot_stride, slots % slot_stride // kv_slots, slots % kv_slots)
    slots = np.arange(group_count * kv_slots)
    key_order = jnp.asarray(order_of(slots // kv_slots, 0, slots % kv_slots), jnp.int32)
    block_groups = max(1, min(group_count, 256 // slot_stride))
    while group_count % block_groups:
        block_groups -= 1
    block_rows = block_groups * slot_stride
    query_order = jnp.asarray(query_order, jnp.int32).reshape(-1, block_rows)

    def far(cache):
        return pltpu.with_memory_space_constraint(cache[0], pltpu.MemorySpace.HBM)

    near = pl.pallas_call(
        functools.partial(stage_kernel, inner, capacity, kv_slots),
        out_shape=(
            jax.ShapeDtypeStruct(cache_keys.shape[1:], cache_keys.dtype),
            jax.ShapeDtypeStruct((H, cache_rows), jnp.float32),
            jax.ShapeDtypeStruct((group_count * kv_slots, H), jnp.float32),
            jax.ShapeDtypeStruct((group_count * kv_slots, 1), jnp.int32),
            jax.ShapeDtypeStruct(query_order.shape, jnp.int32),
        ),
        in_specs=[smem_spec, vmem_spec, hbm_spec] + [vmem_spec] * (5 + group_count),
        out_specs=[vmem_spec] * 5,
        scratch_shapes=[
            pltpu.VMEM((group_count * kv_slots, head_width), jnp.float32),
            pltpu.SemaphoreType.DMA(()),
        ],
        compiler_params=grant(cache_keys),
        name="stage",
    )(
        cache_length,
        token,
        far(cache_keys),
        cache_bucket,
        time_bias.T,
        key_order[:, None],
        query_order,
        base,
        *metas,
    )

    partials = pl.pallas_call(
        functools.partial(
            attend_kernel, slot_stride, kv_slots, block_groups, 0.5 * head_width**-0.5
        ),
        out_shape=jax.ShapeDtypeStruct((device_count, capacity * H, head_width), jnp.bfloat16),
        in_specs=[vmem_spec] * 2 + [hbm_spec] + [vmem_spec] * 4,
        out_specs=vmem_spec,
        scratch_shapes=[
            pltpu.VMEM((block_rows * H, head_width), jnp.float32),
            pltpu.VMEM(cache_values.shape[1:], cache_values.dtype),
            pltpu.VMEM((H, block_rows, cache_rows), jnp.bfloat16),
            pltpu.SemaphoreType.DMA(()),
        ],
        compiler_params=grant(arrived, cache_keys, cache_values, query_order),
        name="attend",
    )(arrived, near[0], far(cache_values), *near[1:])

    returned = lax.all_to_all(partials, AXES, split_axis=0, concat_axis=0, tiled=True)
    contexts = jnp.arange(context_count, dtype=jnp.int32)[:, None]
    places = (owners[None, :] * context_count + contexts) * capacity + ranking[None, :]
    return pl.pallas_call(
        functools.partial(finish_kernel, inner, context_count),
        out_shape=jax.ShapeDtypeStruct((row_count, width), jnp.bfloat16),
        in_specs=[smem_spec] + [vmem_spec] * (H + 2),
        out_specs=vmem_spec,
        scratch_shapes=[
            pltpu.VMEM((row_count * H, head_width), jnp.float32),
            pltpu.VMEM((row_count, width), jnp.bfloat16),
        ],
        compiler_params=grant(returned, norm_gain),
        name="finish",
    )(
        places,
        *gates,
        returned.reshape(device_count * capacity, H, head_width),
        norm_gain[None, :],
    )


def solution(mesh):
    return jax.shard_map(
        shards,
        mesh=mesh,
        in_specs=(
            P(AXES, None),
            P(AXES, None),
            P(AXES),
            P("users", None),
            P(),
            P("users", None),
            P("users", "ctx", None),
            P("users", "ctx", None),
            P("users"),
            P("users", "ctx"),
            P(),
            P(),
        ),
        out_specs=P(AXES, None),
        check_vma=False,
    )
```

```python
import functools

import jax
import jax.numpy as jnp
import numpy as np
from jax import lax
from jax.experimental import pallas as pl
from jax.experimental.pallas import tpu as pltpu
from jax.sharding import PartitionSpec as P

H = 8
AXES = ("users", "ctx")
NORM_EPSILON = 1e-05
DEAD = -1e30
LAG = 6
VMEM = pltpu.MemorySpace.VMEM
SMEM = pltpu.MemorySpace.SMEM


def round_up(value, step):
    return -(-value // step) * step


def seat(inner, context_count):
    return lax.axis_index("users") % inner * context_count + lax.axis_index("ctx")


def grant(*arrays):
    held = sum(int(np.prod(a.shape)) * a.dtype.itemsize for a in arrays)
    return pltpu.CompilerParams(vmem_limit_bytes=min(60 << 20, 2 * held + (6 << 20)))


def pick_columns(inner, context_count, head_width, context, matrix_ref, columns_ref, skip=0):
    owner_count, _, picked = columns_ref.shape
    blocks = picked // head_width
    width = matrix_ref.shape[1] // (blocks + skip)
    for turn in range(inner):
        for block in range(blocks):
            start = (skip + block) * width + (turn * context_count + context) * head_width
            piece = matrix_ref[:, pl.ds(pl.multiple_of(start, head_width), head_width)]
            for first in range(0, owner_count, inner):
                lanes = slice(block * head_width, (block + 1) * head_width)
                columns_ref[first + turn, :, lanes] = piece


def prepare_kernel(events_ref, owner_ref, bucket_ref, packed_ref):
    rows, width = events_ref.shape
    head_width = packed_ref.shape[1] - width
    across = owner_ref[...].astype(jnp.float32)
    owners = jnp.broadcast_to(across, (head_width, rows)).T
    lane = lax.broadcasted_iota(jnp.int32, (rows, rows), 1)
    line = lax.broadcasted_iota(jnp.int32, (rows, rows), 0)
    earlier = (across == owners[:, :1]) & (lane < line)
    ranking = jnp.sum(jnp.where(earlier, 1.0, 0.0), axis=1, keepdims=True)
    buckets = jnp.broadcast_to(bucket_ref[...].astype(jnp.float32), (head_width, rows)).T
    lanes = lax.broadcasted_iota(jnp.int32, (rows, head_width), 1)
    meta = jnp.where(lanes == 0, owners, jnp.where(lanes == 1, ranking, buckets))
    packed_ref[:, :width] = events_ref[...]
    packed_ref[:, width:] = jnp.where(lanes < 3, meta, 0.0).astype(jnp.bfloat16)


def cross_columns_kernel(inner, context_count, head_width, matrix_ref, columns_ref):
    context = lax.axis_index("ctx")
    pick_columns(inner, context_count, head_width, context, matrix_ref, columns_ref)


def spread_columns_kernel(
    inner, context_count, head_width, matrix_ref, columns_ref, *refs
):
    context, user = lax.axis_index("ctx"), lax.axis_index("users")
    pick_columns(inner, context_count, head_width, context, matrix_ref, columns_ref, skip=1)
    half = len(refs) // 2
    for turn in range(half):
        for own, ref in ((user, refs[turn]), (user ^ 1, refs[half + turn])):
            seat = (own & (inner - 1)) ^ (2 * turn & (inner - 1))
            start = (seat * context_count + context) * head_width
            ref[...] = matrix_ref[:, pl.ds(pl.multiple_of(start, head_width), head_width)]


def pair_kernel(*refs):
    count = len(refs) // 3
    rows = refs[0].shape[0]
    mine = lax.axis_index("users") & 1
    for turn in range(count):
        out_ref = refs[2 * count + turn]
        out_ref[pl.ds(pl.multiple_of(mine * rows, rows), rows), :] = refs[turn][...]
        out_ref[pl.ds(pl.multiple_of((1 - mine) * rows, rows), rows), :] = refs[count + turn][...]


def gate_kernel(inner, context_count, crossed_ref, *refs):
    head_count = H
    pieces = refs[: -head_count - 3]
    outs = refs[-head_count - 3 : -3]
    rows_ref, weights_ref, sem = refs[-3:]
    copy = pltpu.make_async_copy(crossed_ref, rows_ref, sem)
    copy.start()
    me, pair = seat(inner, context_count), lax.axis_index("users") >> 1
    depth = pieces[0].shape[0]
    for far, piece in enumerate(pieces):
        weights_ref[pl.ds(pl.multiple_of((pair ^ far) * depth, depth), depth), :] = piece[...]
    copy.wait()
    weights = weights_ref[...]
    rows = outs[0].shape[0]
    for mask in range(head_count):
        source = pl.ds(pl.multiple_of((me ^ mask) * rows, rows), rows)
        half = 0.5 * jnp.dot(rows_ref[source, :], weights, preferred_element_type=jnp.float32)
        outs[mask][...] = (half * (1.0 + jnp.tanh(half))).astype(jnp.bfloat16)


def cross_kernel(inner, context_count, *refs):
    head_count = H
    pieces = refs[:head_count]
    matrix_ref, bias_ref, crossed_ref, turned_ref, meta_ref = refs[head_count:]
    me = seat(inner, context_count)
    rows = pieces[0].shape[0]
    width = bias_ref.shape[1]
    head_width = width // head_count
    columns = pl.ds(pl.multiple_of(me * head_width, head_width), head_width)
    matrix = matrix_ref[...]
    bias = bias_ref[:, columns]
    for mask in range(head_count):
        piece = pieces[mask]
        target = pl.ds(pl.multiple_of((me ^ mask) * rows, rows), rows)
        crossing = jnp.dot(piece[:, :width], matrix, preferred_element_type=jnp.float32)
        source = piece[:, columns].astype(jnp.float32)
        crossed_ref[target, :] = (source * (crossing + bias) + source).astype(jnp.bfloat16)
        meta_ref[target, :] = piece[:, width:].astype(jnp.float32)
    turned_ref[...] = meta_ref[...].T[: turned_ref.shape[0], :]


def project_kernel(inner, context_count, slot_stride, kv_slots, chunk_users, *refs):
    head_count = H
    pieces = refs[:head_count]
    matrix_ref, meta_ref, base_ref = refs[head_count : head_count + 3]
    token_ref, far_rows_ref, out_ref, rows_ref, send_ref, sems = refs[head_count + 3 :]
    token_ref[...] = jnp.zeros_like(token_ref)
    me = seat(inner, context_count)
    head_width = pieces[0].shape[1]
    for mask in range(head_count):
        columns = pl.ds(pl.multiple_of((me ^ mask) * head_width, head_width), head_width)
        rows_ref[:, columns] = pieces[mask][...]
    copy = pltpu.make_async_copy(rows_ref, far_rows_ref, sems.at[0])
    copy.start()
    started = [copy]
    owner = meta_ref[0:1, :].astype(jnp.int32)
    rank = meta_ref[1:2, :].astype(jnp.int32)
    slot_of_row = owner * slot_stride + rank + base_ref[...]
    half = 0.5 * jnp.dot(rows_ref[...], matrix_ref[...], preferred_element_type=jnp.float32)
    activated = (half * (1.0 + jnp.tanh(half))).astype(jnp.bfloat16)
    user_count = send_ref.shape[0] // context_count
    chunk = chunk_users * slot_stride
    for turn, first in enumerate(range(0, user_count, chunk_users)):
        slots = lax.broadcasted_iota(jnp.int32, (chunk, slot_of_row.shape[1]), 0)
        picked = (slots + first * slot_stride == slot_of_row).astype(jnp.float32)
        placed = jnp.dot(
            picked.astype(jnp.bfloat16), activated, preferred_element_type=jnp.float32
        )
        for user in range(chunk_users):
            low = user * slot_stride
            queries = placed[low : low + slot_stride, head_width : 2 * head_width]
            queries = queries.astype(jnp.bfloat16)
            for context in range(context_count):
                target = (first + user) * context_count + context
                start = low + context * kv_slots
                part = placed[start : start + kv_slots]
                send_ref[target, 0:slot_stride, :] = queries
                at = slot_stride
                send_ref[target, at : at + kv_slots, :] = part[:, 2 * head_width :].astype(
                    jnp.bfloat16
                )
                at += kv_slots
                send_ref[target, at : at + kv_slots, :] = part[:, :head_width].astype(
                    jnp.bfloat16
                )
        done = pl.ds(first * context_count, chunk_users * context_count)
        copy = pltpu.make_async_copy(send_ref.at[done], out_ref.at[done], sems.at[turn + 1])
        copy.start()
        started.append(copy)
    for copy in started:
        copy.wait()


def stage_kernel(inner, capacity, kv_slots, length_ref, after_ref, far_ref, *refs):
    bucket_ref, time_bias_ref, key_order_ref, query_order_ref, base_ref = refs[:5]
    metas = refs[5:-7]
    near_ref, cache_bias_ref, new_bias_ref, near_key_order_ref, near_query_order_ref = refs[-7:-2]
    found_ref, sem = refs[-2:]
    copy = pltpu.make_async_copy(far_ref, near_ref, sem)
    copy.start()
    user, context = lax.axis_index("users"), lax.axis_index("ctx")
    table = time_bias_ref[...]
    shape = (table.shape[1], bucket_ref.shape[1])
    levels = lax.broadcasted_iota(jnp.int32, shape, 0)
    picked = jnp.where(levels == bucket_ref[...], 1.0, 0.0)
    bias = jnp.dot(
        table, picked, precision=lax.Precision.HIGHEST, preferred_element_type=jnp.float32
    )
    positions = lax.broadcasted_iota(jnp.int32, bias.shape, 1)
    live = length_ref[0] - context * bias.shape[1]
    cache_bias_ref[...] = jnp.where(positions < live, 0.5 * bias, DEAD)
    group = user // inner
    for mask, meta_ref in enumerate(metas):
        place = meta_ref[1:2, :].astype(jnp.int32) + base_ref[...] - context * kv_slots
        place = jnp.where(meta_ref[0:1, :].astype(jnp.int32) == user, place, -1)
        slots = lax.broadcasted_iota(jnp.int32, (kv_slots, place.shape[1]), 0)
        found = jnp.sum(jnp.where(slots == place, meta_ref[2:3, :], 0.0), axis=1, keepdims=True)
        target = pl.ds(pl.multiple_of((group ^ mask) * kv_slots, 8), kv_slots)
        found_ref[target, :] = jnp.broadcast_to(found, (kv_slots, found_ref.shape[1]))
    levels = lax.broadcasted_iota(jnp.int32, (found_ref.shape[0], table.shape[1]), 1)
    hits = jnp.where(levels == found_ref[:, 0:1].astype(jnp.int32), 1.0, 0.0)
    new_bias_ref[...] = 0.5 * lax.dot_general(
        hits,
        table,
        (((1,), (1,)), ((), ())),
        precision=lax.Precision.HIGHEST,
        preferred_element_type=jnp.float32,
    )
    near_key_order_ref[...] = key_order_ref[...] + context * capacity
    near_query_order_ref[...] = query_order_ref[...]
    copy.wait()


def attend_kernel(
    slot_stride,
    kv_slots,
    block_groups,
    half_scale,
    recv_ref,
    keys_ref,
    far_values_ref,
    cache_bias_ref,
    new_bias_ref,
    key_order_ref,
    query_order_ref,
    out_ref,
    summed_ref,
    values_ref,
    weights_ref,
    sems,
):
    half_width = values_ref.shape[1] // 2
    copies = []
    for side in range(2):
        part = slice(side * half_width, (side + 1) * half_width)
        copies.append(
            pltpu.make_async_copy(far_values_ref.at[:, part], values_ref.at[:, part], sems.at[side])
        )
        copies[-1].start()
    group_count, head_count, _, head_width = recv_ref.shape
    context_count = slot_stride // kv_slots
    inner = head_count // context_count
    capacity = out_ref.shape[1] // head_count
    block_rows = block_groups * slot_stride
    key_count = group_count * kv_slots
    nt = (((1,), (1,)), ((), ()))
    tn = (((0,), (0,)), ((), ()))

    def weigh(first, head):
        columns = slice(head * head_width, (head + 1) * head_width)
        queries = recv_ref[pl.ds(first, block_groups), head, 0:slot_stride, :]
        queries = queries.reshape(block_rows, head_width)
        step = min(256, keys_ref.shape[0])
        for start in range(0, keys_ref.shape[0], step):
            part = slice(start, start + step)
            scores = lax.dot_general(
                queries, keys_ref[part, columns], nt, preferred_element_type=jnp.float32
            )
            half = scores * half_scale + cache_bias_ref[head : head + 1, part]
            weights_ref[head, :, part] = (half * (1.0 + jnp.tanh(half))).astype(jnp.bfloat16)

    def gather(block, first, head):
        columns = slice(head * head_width, (head + 1) * head_width)
        queries = recv_ref[pl.ds(first, block_groups), head, 0:slot_stride, :]
        queries = queries.reshape(block_rows, head_width)
        summed = jnp.dot(
            weights_ref[head], values_ref[:, columns], preferred_element_type=jnp.float32
        )
        at = slot_stride
        new_keys = recv_ref[:, head, at : at + kv_slots, :].reshape(key_count, head_width)
        at += kv_slots
        new_values = recv_ref[:, head, at : at + kv_slots, :].reshape(key_count, head_width)
        new_scores = lax.dot_general(new_keys, queries, nt, preferred_element_type=jnp.float32)
        new_half = new_scores * half_scale + new_bias_ref[:, head : head + 1]
        new_weights = jnp.where(
            key_order_ref[...] <= query_order_ref[pl.ds(block, 1), :],
            new_half * (1.0 + jnp.tanh(new_half)),
            0.0,
        ).astype(jnp.bfloat16)
        summed = summed + lax.dot_general(
            new_weights, new_values, tn, preferred_element_type=jnp.float32
        )
        summed_ref[pl.ds(head, block_rows, stride=head_count), :] = summed

    def one_block(block, waits):
        first = block * block_groups
        lag = LAG
        for head in range(head_count + lag):
            if head < head_count:
                weigh(first, head)
            if waits and head == lag:
                copies[0].wait()
            if waits and head == lag + head_count // 2:
                copies[1].wait()
            if head >= lag:
                gather(block, first, head - lag)
        for group in range(block_groups):
            for context in range(context_count):
                for turn in range(inner):
                    slot = (group * context_count + context) * kv_slots + turn * capacity
                    rows = slice(slot * head_count, (slot + capacity) * head_count)
                    target = (first + group) * head_count + turn * context_count + context
                    out_ref[target] = summed_ref[rows, :].astype(jnp.bfloat16)

    block_count = group_count // block_groups
    if block_count == 1:
        one_block(0, True)
    else:
        for copy in copies:
            copy.wait()

        def step(block, carry):
            one_block(block, False)
            return carry

        lax.fori_loop(0, block_count, step, 0)


def finish_kernel(inner, context_count, place_ref, *refs):
    head_count = H
    gates = refs[:head_count]
    returned_ref, gain_ref, out_ref, tall_ref, gate_ref = refs[head_count:]
    me = seat(inner, context_count)
    rows, width = out_ref.shape
    head_width = width // head_count
    for mask in range(head_count):
        columns = pl.ds(pl.multiple_of((me ^ mask) * head_width, head_width), head_width)
        gate_ref[:, columns] = gates[mask][...]
    for row in range(rows):
        total = returned_ref[place_ref[0, row]].astype(jnp.float32)
        for context in range(1, context_count):
            total = total + returned_ref[place_ref[context, row]].astype(jnp.float32)
        tall_ref[row * head_count : (row + 1) * head_count, :] = total
    attended = jnp.concatenate(
        [tall_ref[pl.ds(head, rows, stride=head_count), :] for head in range(head_count)], axis=1
    )
    center = jnp.mean(attended, axis=1, keepdims=True)
    moved = attended - center
    spread = jnp.mean(jnp.square(moved), axis=1, keepdims=True)
    normed = moved * lax.rsqrt(spread + NORM_EPSILON)
    out_ref[...] = (normed * gain_ref[...] * gate_ref[...].astype(jnp.float32)).astype(jnp.bfloat16)


def shards(
    events,
    owner_id,
    event_bucket,
    cross_weight,
    cross_bias,
    project_weight,
    cache_keys,
    cache_values,
    cache_length,
    cache_bucket,
    time_bias,
    norm_gain,
):
    row_count, width = events.shape
    head_width = width // H
    owner_count = lax.axis_size("users")
    context_count = lax.axis_size("ctx")
    device_count = owner_count * context_count
    inner = H // context_count
    group_count = owner_count // inner
    capacity = max(2, (3 * row_count + 2 * owner_count - 1) // (2 * owner_count))
    kv_slots = round_up(inner * capacity, 8)
    slot_stride = context_count * kv_slots
    cache_rows = cache_keys.shape[1]
    group_rows = H * row_count
    core = context_count if inner > 1 else 0
    blocks = project_weight.shape[1] // width

    def swap(block, mask):
        pairs = [(d, d // H * H + (d % H ^ mask)) for d in range(device_count)]
        return lax.ppermute(block, AXES, pairs)

    def spread(block):
        pieces = [block] + [None] * (H - 1)
        for mask in range(1, H):
            if not mask & core:
                pieces[mask] = swap(block, mask)
        for mask in range(H):
            if mask & core:
                pieces[mask] = swap(pieces[mask ^ core], core)
        return pieces

    owners = owner_id[:, 0]
    positions = jnp.arange(row_count, dtype=jnp.int32)
    earlier = (owners[None, :] == owners[:, None]) & (positions[None, :] < positions[:, None])
    ranking = jnp.sum(earlier.astype(jnp.int32), axis=1)
    vmem_spec = pl.BlockSpec(memory_space=VMEM)
    smem_spec = pl.BlockSpec(memory_space=SMEM)
    hbm_spec = pl.BlockSpec(memory_space=pltpu.MemorySpace.HBM)
    packed_shape = jax.ShapeDtypeStruct((row_count, width + head_width), jnp.bfloat16)
    matrix_rows = cross_weight.shape[0]
    cross_shape = jax.ShapeDtypeStruct((owner_count, matrix_rows, head_width), jnp.bfloat16)
    cross_columns = pl.pallas_call(
        functools.partial(cross_columns_kernel, inner, context_count, head_width),
        out_shape=cross_shape,
        in_specs=[vmem_spec],
        out_specs=vmem_spec,
        name="cross_columns",
    )(cross_weight)
    packed = pl.pallas_call(
        prepare_kernel,
        out_shape=packed_shape,
        in_specs=[vmem_spec] * 3,
        out_specs=vmem_spec,
        name="prepare",
    )(events, owner_id.reshape(1, -1), event_bucket[None, :])
    pieces = spread(packed)
    project_shape = jax.ShapeDtypeStruct(
        (owner_count, matrix_rows, (blocks - 1) * head_width), jnp.bfloat16
    )
    gate_kinds = max(1, inner // 2)
    gate_shape = jax.ShapeDtypeStruct((matrix_rows, head_width), jnp.bfloat16)
    project_columns, *gate_columns = pl.pallas_call(
        functools.partial(spread_columns_kernel, inner, context_count, head_width),
        out_shape=[project_shape] + [gate_shape] * (2 * gate_kinds),
        in_specs=[vmem_spec],
        out_specs=[vmem_spec] * (1 + 2 * gate_kinds),
        compiler_params=grant(project_shape),
        name="columns",
    )(project_weight)

    cross_columns = lax.all_to_all(cross_columns, "users", split_axis=0, concat_axis=0, tiled=True)
    project_columns = lax.all_to_all(
        project_columns, "users", split_axis=0, concat_axis=0, tiled=True
    )
    project_columns = project_columns.reshape(width, (blocks - 1) * head_width)
    cross_columns = cross_columns.reshape(width, head_width)

    def trade(block, mask):
        pairs = [
            (u * context_count + c, (u ^ mask) * context_count + c)
            for u in range(owner_count)
            for c in range(context_count)
        ]
        return lax.ppermute(block, AXES, pairs)

    gate_other = [trade(block, 1) for block in gate_columns[gate_kinds:]]
    gate_pairs = pl.pallas_call(
        pair_kernel,
        out_shape=[jax.ShapeDtypeStruct((2 * matrix_rows, head_width), jnp.bfloat16)]
        * gate_kinds,
        in_specs=[vmem_spec] * (2 * gate_kinds),
        out_specs=[vmem_spec] * gate_kinds,
        compiler_params=grant(project_shape),
        name="pair",
    )(*gate_columns[:gate_kinds], *gate_other)
    gate_pieces = [gate_pairs[0]] + [
        trade(gate_pairs[mask // 2 % gate_kinds], mask) for mask in range(2, owner_count, 2)
    ]

    meta_shape = jax.ShapeDtypeStruct((8, group_rows), jnp.float32)
    crossed, group_meta = pl.pallas_call(
        functools.partial(cross_kernel, inner, context_count),
        out_shape=(
            jax.ShapeDtypeStruct((group_rows, head_width), jnp.bfloat16),
            meta_shape,
        ),
        in_specs=[vmem_spec] * (H + 2),
        out_specs=(vmem_spec, vmem_spec),
        scratch_shapes=[pltpu.VMEM((group_rows, head_width), jnp.float32)],
        compiler_params=grant(*pieces, cross_columns),
        name="cross",
    )(*pieces, cross_columns, cross_bias[None, :])
    crossed_pieces = spread(crossed)
    metas = [group_meta]
    for mask in range(1, group_count):
        pairs = [
            (g * H + member, (g ^ mask) * H + member)
            for g in range(group_count)
            for member in range(H)
        ]
        metas.append(lax.ppermute(group_meta, AXES, pairs))

    shard = np.arange(group_rows) // row_count
    base = ((shard % context_count) * kv_slots + (shard // context_count) * capacity)[None, :]
    message_rows = slot_stride + 2 * kv_slots
    base = jnp.asarray(base, jnp.int32)
    chunk_users = max(1, min(owner_count, 256 // slot_stride))
    while owner_count % chunk_users:
        chunk_users -= 1
    messages = jax.ShapeDtypeStruct((device_count, message_rows, head_width), jnp.bfloat16)
    token, far_rows, outgoing = pl.pallas_call(
        functools.partial(project_kernel, inner, context_count, slot_stride, kv_slots, chunk_users),
        out_shape=[
            jax.ShapeDtypeStruct((8, head_width), jnp.float32),
            pltpu.MemorySpace.HBM((group_rows, width), jnp.bfloat16),
            messages,
        ],
        in_specs=[vmem_spec] * (H + 3),
        out_specs=[vmem_spec] + [hbm_spec] * 2,
        scratch_shapes=[
            pltpu.VMEM((group_rows, width), jnp.bfloat16),
            pltpu.VMEM(messages.shape, messages.dtype),
            pltpu.SemaphoreType.DMA((owner_count // chunk_users + 1,)),
        ],
        compiler_params=grant(*crossed_pieces, project_columns, messages, messages),
        name="project",
    )(*crossed_pieces, project_columns, group_meta, base)
    gates = pl.pallas_call(
        functools.partial(gate_kernel, inner, context_count),
        out_shape=[jax.ShapeDtypeStruct((row_count, head_width), jnp.bfloat16)] * H,
        in_specs=[hbm_spec] + [vmem_spec] * len(gate_pieces),
        out_specs=[vmem_spec] * H,
        scratch_shapes=[
            pltpu.VMEM((group_rows, width), jnp.bfloat16),
            pltpu.VMEM((width, head_width), jnp.bfloat16),
            pltpu.SemaphoreType.DMA(()),
        ],
        compiler_params=grant(far_rows),
        name="gate",
    )(
        pltpu.with_memory_space_constraint(far_rows, pltpu.MemorySpace.HBM),
        *gate_pieces,
    )
    gates = [gates[0]] + [swap(gates[mask], mask) for mask in range(1, H)]

    arrived = lax.all_to_all(outgoing, AXES, split_axis=0, concat_axis=0, tiled=True)
    arrived = arrived.reshape(group_count, H, message_rows, head_width)

    def order_of(group, context, rest):
        member = rest // capacity * context_count + context
        return (group * H + member) * capacity + rest % capacity

    slots = np.arange(group_count * slot_stride)
    query_order = order_of(slots // slot_stride, slots % slot_stride // kv_slots, slots % kv_slots)
    slots = np.arange(group_count * kv_slots)
    key_order = jnp.asarray(order_of(slots // kv_slots, 0, slots % kv_slots), jnp.int32)
    block_groups = max(1, min(group_count, 256 // slot_stride))
    while group_count % block_groups:
        block_groups -= 1
    block_rows = block_groups * slot_stride
    query_order = jnp.asarray(query_order, jnp.int32).reshape(-1, block_rows)

    def far(cache):
        return pltpu.with_memory_space_constraint(cache[0], pltpu.MemorySpace.HBM)

    near = pl.pallas_call(
        functools.partial(stage_kernel, inner, capacity, kv_slots),
        out_shape=(
            jax.ShapeDtypeStruct(cache_keys.shape[1:], cache_keys.dtype),
            jax.ShapeDtypeStruct((H, cache_rows), jnp.float32),
            jax.ShapeDtypeStruct((group_count * kv_slots, H), jnp.float32),
            jax.ShapeDtypeStruct((group_count * kv_slots, 1), jnp.int32),
            jax.ShapeDtypeStruct(query_order.shape, jnp.int32),
        ),
        in_specs=[smem_spec, vmem_spec, hbm_spec] + [vmem_spec] * (5 + group_count),
        out_specs=[vmem_spec] * 5,
        scratch_shapes=[
            pltpu.VMEM((group_count * kv_slots, head_width), jnp.float32),
            pltpu.SemaphoreType.DMA(()),
        ],
        compiler_params=grant(cache_keys),
        name="stage",
    )(
        cache_length,
        token,
        far(cache_keys),
        cache_bucket,
        time_bias.T,
        key_order[:, None],
        query_order,
        base,
        *metas,
    )

    partials = pl.pallas_call(
        functools.partial(
            attend_kernel, slot_stride, kv_slots, block_groups, 0.5 * head_width**-0.5
        ),
        out_shape=jax.ShapeDtypeStruct((device_count, capacity * H, head_width), jnp.bfloat16),
        in_specs=[vmem_spec] * 2 + [hbm_spec] + [vmem_spec] * 4,
        out_specs=vmem_spec,
        scratch_shapes=[
            pltpu.VMEM((block_rows * H, head_width), jnp.float32),
            pltpu.VMEM(cache_values.shape[1:], cache_values.dtype),
            pltpu.VMEM((H, block_rows, cache_rows), jnp.bfloat16),
            pltpu.SemaphoreType.DMA((2,)),
        ],
        compiler_params=grant(arrived, cache_keys, cache_values, query_order),
        name="attend",
    )(arrived, near[0], far(cache_values), *near[1:])

    returned = lax.all_to_all(partials, AXES, split_axis=0, concat_axis=0, tiled=True)
    contexts = jnp.arange(context_count, dtype=jnp.int32)[:, None]
    places = (owners[None, :] * context_count + contexts) * capacity + ranking[None, :]
    return pl.pallas_call(
        functools.partial(finish_kernel, inner, context_count),
        out_shape=jax.ShapeDtypeStruct((row_count, width), jnp.bfloat16),
        in_specs=[smem_spec] + [vmem_spec] * (H + 2),
        out_specs=vmem_spec,
        scratch_shapes=[
            pltpu.VMEM((row_count * H, head_width), jnp.float32),
            pltpu.VMEM((row_count, width), jnp.bfloat16),
        ],
        compiler_params=grant(returned, norm_gain),
        name="finish",
    )(
        places,
        *gates,
        returned.reshape(device_count * capacity, H, head_width),
        norm_gain[None, :],
    )


def solution(mesh):
    return jax.shard_map(
        shards,
        mesh=mesh,
        in_specs=(
            P(AXES, None),
            P(AXES, None),
            P(AXES),
            P("users", None),
            P(),
            P("users", None),
            P("users", "ctx", None),
            P("users", "ctx", None),
            P("users"),
            P("users", "ctx"),
            P(),
            P(),
        ),
        out_specs=P(AXES, None),
        check_vma=False,
    )
```
